32 devices in a mesh: row: 4 (over y, x), col: 8 (over z, core).
Axes of the slice: x: 2, y: 2, z: 4, core: 2. Of those that a mesh axis runs over, the one named last changes fastest.
Arguments:
- object_tiles: float32 [2, 2, 1024, 2048], P(None, None, 'row', 'col'), may hold values from -5 to 5
- probe_modes: float32 [2, 4, 128, 128], replicated, may hold values from -6 to 6
- offsets: int32 [4, 8, 3, 2], P('row', 'col'), may hold values from 0 to 192
- amplitude: float32 [4, 8, 3, 128, 128], P('row', 'col'), may hold values from 0.2 to 3
Outputs:
- object_grad: float32 [2, 2, 1024, 2048], P(None, None, 'row', 'col')
- probe_new: float32 [2, 4, 128, 128], replicated
The draws below stay inside these ranges and needn't reach their ends.
All inputs are finite; a program needn't handle non-finite values.
Results may differ from the reference program's by a relative error of at most 0.0003.
Values sent between devices are 32-bit elements; how exact they have to be, the bound alone decides.
A program may use at most 64 MiB of HBM per device.

```python
import jax
import jax.numpy as jnp
from jax import lax

TILE = 256
HALO = 32
WIN = 128
MODES = 4
SLICES = 2
SCANS = 3
OBJ_ROWS = 1024
OBJ_COLS = 2048
N_ROW = 4
N_COL = 8


def plant(entries, key, least, top_value):
    shape = entries.shape
    index_at = [jax.random.randint(jax.random.fold_in(key, axis), (), 0, shape[axis]) for axis in range(len(shape))]
    entries = entries.at[tuple(index_at)].set(least)
    longest = shape.index(max(shape))
    index_at[longest] = (index_at[longest] + 1) % shape[longest]
    return entries.at[tuple(index_at)].set(top_value)


def block_scale(stream_key, dims, shards, low, top_value):
    def one(position, shards_of):
        heights = jax.random.uniform(jax.random.fold_in(jax.random.fold_in(stream_key, 6), position), (shards_of,), jnp.float32, low / len(shards), top_value / len(shards))
        return jnp.repeat(jnp.exp(heights), dims[position] // shards_of).reshape((-1,) + (1,) * (len(dims) - position - 1))

    gain = one(*shards[0])
    for cut in shards[1:]:
        gain = gain * one(*cut)
    return gain


def centred(own_key, extent, spread, limit, cuts=(), held_as=jnp.bfloat16):
    drawn = spread * jax.random.normal(own_key, extent, jnp.float32)
    if cuts:
        drawn = drawn * block_scale(own_key, extent, cuts, -0.22, 0.18)
    return jnp.clip(drawn, -limit, limit).astype(held_as)


def setup_inputs(seed: int = 0) -> dict:
    splits = jax.random.split(jax.random.key(seed), 5)
    return {
        "object_tiles": centred(splits[0], (2, SLICES, OBJ_ROWS, OBJ_COLS), 0.7, 5.0, ((2, 4), (3, 8)), jnp.float32),
        "probe_modes": centred(splits[1], (2, MODES, WIN, WIN), 1.0, 6.0, (), jnp.float32),
        "offsets": plant(jax.random.randint(splits[2], (N_ROW, N_COL, SCANS, 2), 0, TILE + 2 * HALO - WIN + 1), jax.random.fold_in(splits[2], 1), 0, TILE + 2 * HALO - WIN).astype(jnp.int32),
        "amplitude": jnp.clip(0.2 + 2.8 * jax.random.uniform(splits[3], (N_ROW, N_COL, SCANS, WIN, WIN), jnp.float32) ** block_scale(splits[3], (N_ROW, N_COL, SCANS, WIN, WIN), ((0, 4), (1, 8)), -0.2, 0.2), 0.2, 3.0),
    }


PROP = 0.002
SHIFT_AMP = 0.5
STEP_SIZE = 0.5
EPSILON = 1e-06
HIGH = lax.Precision.HIGHEST

def tables():
    counter = jnp.arange(WIN, dtype=jnp.int32)
    product = counter[:, None] * counter[None, :] % WIN
    angles = product.astype(jnp.float32) * (2.0 * jnp.pi / WIN)
    scale_factor = 1.0 / jnp.sqrt(jnp.float32(WIN))
    cos_table = jnp.cos(angles) * scale_factor
    sin_table = jnp.sin(angles) * scale_factor
    frequency = ((counter + WIN // 2) % WIN - WIN // 2).astype(jnp.float32)
    phase_map = -PROP * (frequency[:, None] ** 2 + frequency[None, :] ** 2)
    return (cos_table, sin_table, jnp.cos(phase_map), jnp.sin(phase_map))

def matprod(left_op, right_op):
    return jnp.matmul(left_op, right_op, precision=HIGH)

def transform(wave_real, wave_imag, sign_value, cos_table, sin_table):
    first_real = matprod(cos_table, wave_real) + sign_value * matprod(sin_table, wave_imag)
    first_imag = matprod(cos_table, wave_imag) - sign_value * matprod(sin_table, wave_real)
    second_real = matprod(first_real, cos_table) + sign_value * matprod(first_imag, sin_table)
    second_imag = matprod(first_imag, cos_table) - sign_value * matprod(first_real, sin_table)
    return (second_real, second_imag)

def position_loss(window, probe_field, measured, table_set):
    cos_table, sin_table, prop_cos, prop_sin = table_set
    probe_real = probe_field[0]
    probe_imag = probe_field[1]
    wave_real = probe_real * window[0, 0] - probe_imag * window[1, 0]
    wave_imag = probe_real * window[1, 0] + probe_imag * window[0, 0]
    for layer_no in range(1, SLICES):
        wave_real, wave_imag = transform(wave_real, wave_imag, 1.0, cos_table, sin_table)
        turned_real = wave_real * prop_cos - wave_imag * prop_sin
        turned_imag = wave_real * prop_sin + wave_imag * prop_cos
        wave_real, wave_imag = transform(turned_real, turned_imag, -1.0, cos_table, sin_table)
        slice_real = window[0, layer_no]
        slice_imag = window[1, layer_no]
        wave_real, wave_imag = (wave_real * slice_real - wave_imag * slice_imag, wave_real * slice_imag + wave_imag * slice_real)
    far_real, far_imag = transform(wave_real, wave_imag, 1.0, cos_table, sin_table)
    intensity = lax.optimization_barrier(jnp.sum(far_real * far_real + far_imag * far_imag, axis=0))
    return jnp.sum((jnp.sqrt(intensity + SHIFT_AMP) - measured) ** 2)

def update_probe(probe_field, gradient):
    mean_square = jnp.sum(gradient * gradient) / (2 * MODES * WIN * WIN)
    return probe_field - STEP_SIZE * gradient / jnp.sqrt(mean_square + EPSILON)

def reference(object_tiles, probe_modes, offsets, amplitude):
    table_set = tables()
    obj_rows = object_tiles.shape[2]
    obj_cols = object_tiles.shape[3]
    flat_offsets = offsets.reshape(-1, 2)
    flat_amp = amplitude.reshape(-1, WIN, WIN)
    numbers = jnp.arange(flat_offsets.shape[0], dtype=jnp.int32)
    window_span = jnp.arange(WIN, dtype=jnp.int32)

    def total_loss(tiles_field, probe_field):

        def step_fn(loss_acc, scan_item):
            number, shift_pair, measured = scan_item
            grid_row = number // (N_COL * SCANS)
            grid_col = number // SCANS % N_COL
            row_start = grid_row * TILE - HALO + shift_pair[0]
            col_start = grid_col * TILE - HALO + shift_pair[1]
            row_index = ((row_start + window_span) % obj_rows).astype(jnp.int32)
            col_index = ((col_start + window_span) % obj_cols).astype(jnp.int32)
            window = jnp.take(jnp.take(tiles_field, row_index, axis=2), col_index, axis=3)
            return (loss_acc + position_loss(window, probe_field, measured, table_set), None)
        loss_sum, _ = lax.scan(step_fn, jnp.zeros((), jnp.float32), (numbers, flat_offsets, flat_amp))
        return loss_sum
    grad_tiles, grad_probe = jax.grad(total_loss, argnums=(0, 1))(object_tiles, probe_modes)
    return (grad_tiles, update_probe(probe_modes, grad_probe))
```

```python
import functools

import jax
import jax.numpy as jnp
import numpy as np
from jax import lax
from jax.experimental import pallas as pl
from jax.experimental.pallas import tpu as pltpu
from jax.sharding import PartitionSpec as P

HALO = 32
PROP = 0.002
SHIFT_AMP = 0.5
STEP_SIZE = 0.5
EPSILON = 1e-06
LANES = 128
SUB = 8
MESH = pl.DeviceIdType.MESH
F32 = jnp.float32
BF16 = jnp.bfloat16


def tables(win):
    k = np.arange(win)
    c = np.exp(-2j * np.pi * (k[:, None] * k[None, :] % win) / win) / np.sqrt(win)
    freq = (k + win // 2) % win - win // 2
    kern = np.conj(c) @ np.diag(np.exp(-1j * PROP * freq**2)) @ c
    out = []
    for m in (c, np.conj(c), kern, np.conj(kern)):
        full = np.block([[m.real, m.imag], [-m.imag, m.real]])
        high = full.astype(np.float32).astype(jnp.bfloat16)
        low = (full - high.astype(np.float64)).astype(np.float32).astype(jnp.bfloat16)
        out += [high, low]
    return np.stack(out)


FWD, INV, KER, KER_INV = 0, 1, 2, 3


def split(x):
    high = x.astype(BF16)
    return high, (x - high.astype(F32)).astype(BF16)


def dot(a, b):
    return jnp.dot(a, b, preferred_element_type=F32)


def right(x, tab, which):
    high, low = split(x)
    return dot(high, tab[2 * which]) + (
        dot(low, tab[2 * which]) + dot(high, tab[2 * which + 1])
    )


def left(x, tab, which):
    high, low = split(x)
    which = which ^ 1
    return dot(tab[2 * which], high) + (
        dot(tab[2 * which], low) + dot(tab[2 * which + 1], high)
    )


def swap(y):
    w = y.shape[0] // 2
    top = jnp.concatenate([y[:w, :w], y[w:, :w]], axis=1)
    low = jnp.concatenate([y[:w, w:], y[w:, w:]], axis=1)
    return jnp.concatenate([top, low], axis=0)


def twice(x, axis):
    return jnp.concatenate([x, x], axis=axis)


def lane(rows):
    return lax.broadcasted_iota(jnp.int32, (rows, LANES), 1)


FOLD = HALO // 2


def fold(get, rows, first):
    at = lane(rows // 2)
    out = None
    for part in range(2):
        x = get(part)
        for h in range(2):
            low = HALO * (2 * h + part)
            block = jnp.concatenate(
                [x[HALO * b + FOLD * h : HALO * b + FOLD * (h + 1)] for b in range(rows // HALO)],
                axis=0,
            )
            shift = (low - first) % LANES
            block = pltpu.roll(block, shift, 1) if shift else block
            keep = (at >= low) & (at < low + HALO)
            out = jnp.where(keep, block, 0.0 if out is None else out)
    return out


def unfold(x, part, first):
    halves = []
    for h in range(2):
        shift = (first - HALO * (2 * h + part)) % LANES
        halves.append(pltpu.roll(x, shift, 1) if shift else x)
    return jnp.concatenate(
        [
            halves[h][FOLD * b : FOLD * (b + 1)]
            for b in range(x.shape[0] // FOLD)
            for h in range(2)
        ],
        axis=0,
    )


def remote(src, dst, ssem, rsem, to):
    copy = pltpu.make_async_remote_copy(
        src_ref=src,
        dst_ref=dst,
        send_sem=ssem,
        recv_sem=rsem,
        device_id=to,
        device_id_type=MESH,
    )
    copy.start()
    return copy


def fused_kernel(
    sizes,
    off_ref,
    obj_hbm,
    probe_hbm,
    amp_hbm,
    tab_hbm,
    grad_ref,
    new_ref,
    ext_0,
    ext_1,
    probe,
    amp,
    tab,
    winds,
    wave,
    far,
    factor,
    gobj,
    gprobe,
    zpad,
    acc,
    pack_l,
    pack_r,
    halo_l,
    halo_r,
    from_top,
    from_bot,
    edge_l,
    edge_r,
    from_l,
    from_r,
    half_in,
    half_sum,
    r_parts,
    z_parts,
    total,
    in_sem,
    h_send,
    h_recv,
    g_send,
    g_recv,
    pair_send,
    pair_recv,
    r_send,
    r_recv,
    z_send,
    z_recv,
    ag_send,
    ag_recv,
    fw_send,
    fw_recv,
):
    n_row, n_col, win, scans, chunks = sizes
    n_z = n_col // 2
    ext = (ext_0, ext_1)
    tile = grad_ref.shape[2]
    tall = tile + 2 * HALO
    nt = tile // LANES
    pad = tall - win
    my_r, my_c = lax.axis_index("row"), lax.axis_index("col")

    def at(dr, dc):
        return lax.rem(my_r + dr % n_row, n_row), lax.rem(my_c + dc % n_col, n_col)

    loads = []
    for lay in range(2):
        for part in range(2):
            for t in range(nt):
                loads.append(
                    pltpu.make_async_copy(
                        obj_hbm.at[part, lay, :, pl.ds(t * LANES, LANES)],
                        ext[lay].at[part, t, pl.ds(HALO, tile), :],
                        in_sem.at[len(loads)],
                    )
                )
    per_lay = len(loads) // 2
    for src, dst in ((probe_hbm, probe), (tab_hbm, tab), (amp_hbm, amp)):
        loads.append(pltpu.make_async_copy(src, dst, in_sem.at[len(loads)]))
    for load in loads:
        load.start()
    barrier = pltpu.get_barrier_semaphore()
    mates = {(dr % n_row, dc % n_col) for dr in (-1, 0, 1) for dc in (-1, 0, 1)}
    mates |= {(k, 0) for k in range(n_row)} | {(0, 2 * k) for k in range(n_z)}
    mates.discard((0, 0))
    for mate in sorted(mates):
        pl.semaphore_signal(barrier, inc=1, device_id=at(*mate), device_id_type=MESH)

    head, tail = pl.ds(0, FOLD), pl.ds((tile - HALO) // 2, FOLD)
    mid, after = pl.ds(FOLD, tile // 2), pl.ds(FOLD + tile // 2, FOLD)

    def pack(lay):
        for load in loads[lay * per_lay : (lay + 1) * per_lay]:
            load.wait()
        own = pl.ds(HALO, tile)
        pack_l[lay] = fold(lambda part: ext[lay][part, 0, own, :], tile, 0)
        pack_r[lay] = fold(lambda part: ext[lay][part, nt - 1, own, :], tile, LANES - HALO)

    def halo_start(lay):
        e, left_in, right_in = ext[lay], halo_l.at[lay], halo_r.at[lay]
        pl_, pr_ = pack_l.at[lay], pack_r.at[lay]
        own = pl.ds(0, nt)
        plan = [
            (e.at[:, own, pl.ds(tile, HALO)], e.at[:, own, pl.ds(0, HALO)], (1, 0)),
            (e.at[:, own, pl.ds(HALO, HALO)], e.at[:, own, pl.ds(HALO + tile, HALO)], (-1, 0)),
            (pr_, left_in.at[mid], (0, 1)),
            (pl_, right_in.at[mid], (0, -1)),
            (pr_.at[tail], left_in.at[head], (1, 1)),
            (pr_.at[head], left_in.at[after], (-1, 1)),
            (pl_.at[tail], right_in.at[head], (1, -1)),
            (pl_.at[head], right_in.at[after], (-1, -1)),
        ]
        return [
            remote(src, dst, h_send.at[lay, i], h_recv.at[lay, i], at(*to))
            for i, (src, dst, to) in enumerate(plan)
        ]

    def halo_end(lay, copies):
        for copy in copies:
            copy.wait_recv()
        for part in range(2):
            near = unfold(halo_r[lay], part, 0)
            distant = unfold(halo_l[lay], part, LANES - HALO)
            x = lane(tall)
            ext[lay][part, nt, pl.ds(0, tall), :] = jnp.where(
                x < HALO, near, jnp.where(x >= LANES - HALO, distant, 0.0)
            )

    def spot(s):
        row = off_ref[0, 0, 0, s]
        col = off_ref[0, 0, 1, s] - HALO
        col = jnp.where(col < 0, col + (nt + 1) * LANES, col)
        first = lax.div(col, LANES)
        second = jnp.where(first == nt, 0, first + 1)
        return row, first, second, col - first * LANES

    def windows(lay):
        @pl.loop(0, scans)
        def _(s):
            row, first, second, rem = spot(s)
            for part in range(2):
                a = ext[lay][part, first, pl.ds(row, win), :]
                b = ext[lay][part, second, pl.ds(row, win), :]
                block = jnp.where(lane(win) >= rem, a, b)
                winds[s, 2 * part + lay] = pltpu.roll(block, lax.rem(LANES - rem, LANES), 1)

    pack(0)
    pl.semaphore_wait(barrier, len(mates))
    halo_0 = halo_start(0)
    pack(1)
    halo_1 = halo_start(1)
    gprobe[...] = jnp.zeros_like(gprobe)
    gobj[...] = jnp.zeros_like(gobj)
    zpad[...] = jnp.zeros_like(zpad)
    for load in loads[2 * per_lay :]:
        load.wait()
    halo_end(0, halo_0)
    windows(0)

    @pl.loop(0, scans)
    def _(s):
        or_, oi_ = winds[s, 0], winds[s, 2]
        for p in range(2):
            rows = []
            for m in range(2):
                pr, pi = probe[0, 2 * p + m], probe[1, 2 * p + m]
                rows.append(
                    jnp.concatenate([pr * or_ - pi * oi_, pr * oi_ + pi * or_], axis=1)
                )
            psi = jnp.concatenate(rows, axis=0)
            wave[s, p] = left(swap(right(psi, tab, KER)), tab, KER)

    halo_end(1, halo_1)
    windows(1)

    @pl.loop(0, scans)
    def _(s):
        power = None
        for p in range(2):
            w = wave[s, p]
            wr, wi = w[:win], w[win:]
            o1r, o1i = twice(winds[s, 1], 1), twice(winds[s, 3], 1)
            psi = jnp.concatenate([wr * o1r - wi * o1i, wr * o1i + wi * o1r], axis=0)
            psi = right(swap(left(psi, tab, FWD)), tab, FWD)
            far[s, p] = psi
            sq = psi * psi
            part_sum = (sq[:win, :win] + sq[:win, win:]) + (sq[win:, :win] + sq[win:, win:])
            power = part_sum if power is None else power + part_sum
        root = jnp.sqrt(power + SHIFT_AMP)
        factor[s] = 2.0 * (root - amp[0, 0, s]) / root

    def first_half(p, s):
        g = far[s, p] * twice(twice(factor[s], 0), 1)
        g = left(swap(right(g, tab, INV)), tab, INV)
        w = wave[s, p]
        gr, gi, wr, wi = g[:win], g[win:], w[:win], w[win:]
        re = wr * gr + wi * gi
        im = wr * gi - wi * gr
        gobj[1, 0, s] += re[:, :win] + re[:, win:]
        gobj[1, 1, s] += im[:, :win] + im[:, win:]
        o1r, o1i = twice(winds[s, 1], 1), twice(winds[s, 3], 1)
        far[s, p] = jnp.concatenate([o1r * gr + o1i * gi, o1r * gi - o1i * gr], axis=0)

    def second_half(p, s):
        g = right(swap(left(far[s, p], tab, KER_INV)), tab, KER_INV)
        o0r, o0i = winds[s, 0], winds[s, 2]
        re = im = None
        for m in range(2):
            gr, gi = g[m * win : (m + 1) * win, :win], g[m * win : (m + 1) * win, win:]
            pr, pi = probe[0, 2 * p + m], probe[1, 2 * p + m]
            a = pr * gr + pi * gi
            b = pr * gi - pi * gr
            re, im = (a, b) if re is None else (re + a, im + b)
            base = (2 * p + m) * 2 * win
            gprobe[pl.ds(base, win)] += o0r * gr + o0i * gi
            gprobe[pl.ds(base + win, win)] += o0r * gi - o0i * gr
        gobj[0, 0, s] += re
        gobj[0, 1, s] += im

    def place(lay):
        starts = []
        for s in range(scans):
            row, first, second, rem = spot(s)
            starts.append(pad - row)
            where = jnp.where(lane(win) >= rem, first, second)
            for part in range(2):
                block = pltpu.roll(gobj[lay, part, s], rem, 1)
                for t in range(nt + 1):
                    zpad[s, part, t, pl.ds(pad, win), :] = jnp.where(where == t, block, 0.0)
        for part in range(2):
            for t in range(nt + 1):
                value = None
                for s in range(scans):
                    block = zpad[s, part, t, pl.ds(starts[s], tall), :]
                    value = block if value is None else value + block
                acc[lay, part, t] = value

    def grads_start(lay):
        a, er, el = acc.at[lay], edge_r.at[lay], edge_l.at[lay]
        fl, fr = from_l.at[lay], from_r.at[lay]
        edge_r[lay] = fold(lambda part: acc[lay, part, nt], tall, 0)
        edge_l[lay] = fold(lambda part: acc[lay, part, nt], tall, LANES - HALO)
        own = pl.ds(0, nt)
        plan = [
            (a.at[:, own, pl.ds(0, HALO)], from_bot.at[lay], (-1, 0)),
            (a.at[:, own, pl.ds(HALO + tile, HALO)], from_top.at[lay], (1, 0)),
            (er.at[mid], fl.at[mid], (0, 1)),
            (el.at[mid], fr.at[mid], (0, -1)),
            (er.at[head], fl.at[after], (-1, 1)),
            (er.at[after], fl.at[head], (1, 1)),
            (el.at[head], fr.at[after], (-1, -1)),
            (el.at[after], fr.at[head], (1, -1)),
        ]
        return [
            remote(src, dst, g_send.at[lay, i], g_recv.at[lay, i], at(*to))
            for i, (src, dst, to) in enumerate(plan)
        ]

    def grads_end(lay, copies):
        for copy in copies:
            copy.wait_recv()
        x = lane(tall)
        for part in range(2):
            for t in range(nt):
                value = acc[lay, part, t, pl.ds(HALO, tile), :]
                top, bot = from_top[lay, part, t], from_bot[lay, part, t]
                for ref, first, edge in ((from_l, 0, 0), (from_r, LANES - HALO, nt - 1)):
                    if t == edge:
                        block = unfold(ref[lay], part, first)
                        block = jnp.where((x >= first) & (x < first + HALO), block, 0.0)
                        value = value + block[HALO : HALO + tile]
                        top = top + block[:HALO]
                        bot = bot + block[HALO + tile :]
                cols = pl.ds(t * LANES, LANES)
                grad_ref[part, lay, pl.ds(0, HALO), cols] = value[:HALO] + top
                grad_ref[part, lay, pl.ds(HALO, tile - 2 * HALO), cols] = value[HALO:-HALO]
                grad_ref[part, lay, pl.ds(tile - HALO, HALO), cols] = value[-HALO:] + bot

    odd = lax.rem(my_c, 2)
    partner = (my_r, my_c + 1 - 2 * odd)
    my_z = lax.div(my_c, 2)

    def span(c):
        start, size = chunks[c]
        half = size // 2
        piece = half // n_row
        return start, half, piece, start // 2, start // 2 // n_row

    def rows_at(start, size):
        return pl.ds(pl.multiple_of(start, SUB), size)

    def row_mate(k):
        return lax.rem(my_r + k, n_row)

    def pair_start(c):
        start, half, piece, hs, ps = span(c)
        return remote(
            gprobe.at[rows_at(start + (1 - odd) * half, half)],
            half_in.at[pl.ds(hs, half)],
            pair_send.at[c],
            pair_recv.at[c],
            partner,
        )

    def r_start(c, pair):
        start, half, piece, hs, ps = span(c)
        pair.wait_recv()
        half_sum[pl.ds(hs, half)] = (
            gprobe[rows_at(start + odd * half, half)] + half_in[pl.ds(hs, half)]
        )
        copies = []
        for k in range(1, n_row):
            q = row_mate(k)
            copies.append(
                remote(
                    half_sum.at[rows_at(hs + q * piece, piece)],
                    r_parts.at[k - 1, pl.ds(ps, piece)],
                    r_send.at[c, k - 1],
                    r_recv.at[c, k - 1],
                    (q, my_c),
                )
            )
        return copies

    def z_start(c, before):
        start, half, piece, hs, ps = span(c)
        for copy in before:
            copy.wait_recv()
        value = half_sum[rows_at(hs + my_r * piece, piece)]
        for k in range(n_row - 1):
            value = value + r_parts[k, pl.ds(ps, piece)]
        z_parts[my_z, pl.ds(ps, piece)] = value
        mine = z_parts.at[my_z, pl.ds(ps, piece)]
        return [
            remote(mine, mine, z_send.at[c, k - 1], z_recv.at[c, k - 1], at(0, 2 * k))
            for k in range(1, n_z)
        ]

    def ag_start(c, before):
        start, half, piece, hs, ps = span(c)
        for copy in before:
            copy.wait_recv()
        value = z_parts[0, pl.ds(ps, piece)]
        for k in range(1, n_z):
            value = value + z_parts[k, pl.ds(ps, piece)]
        own = rows_at(start + odd * half + my_r * piece, piece)
        total[own] = value
        mine = total.at[own]
        copies = [
            remote(mine, mine, ag_send.at[c, k - 1], ag_recv.at[c, k - 1], at(k, 0))
            for k in range(1, n_row)
        ]
        return copies, [remote(mine, mine, fw_send.at[c, 0], fw_recv.at[c, 0], partner)]

    def fw_start(c, copies, forwards):
        start, half, piece, hs, ps = span(c)
        for k in range(1, n_row):
            copies[k - 1].wait_recv()
            q = lax.rem(my_r + n_row - k, n_row)
            got = total.at[rows_at(start + odd * half + q * piece, piece)]
            forwards.append(remote(got, got, fw_send.at[c, k], fw_recv.at[c, k], partner))

    @pl.loop(0, scans)
    def _(s):
        first_half(0, s)
        second_half(0, s)

    early, late = range(len(chunks) // 2), range(len(chunks) // 2, len(chunks))
    every = range(len(chunks))
    pair, row, zed, gat = {}, {}, {}, {}
    for c in early:
        pair[c] = pair_start(c)

    @pl.loop(0, scans)
    def _(s):
        first_half(1, s)

    for c in early:
        row[c] = r_start(c, pair[c])
    place(1)
    copies_1 = grads_start(1)

    @pl.loop(0, scans)
    def _(s):
        second_half(1, s)

    for c in late:
        pair[c] = pair_start(c)
    place(0)
    for c in late:
        row[c] = r_start(c, pair[c])
    copies_0 = grads_start(0)
    for c in early:
        zed[c] = z_start(c, row[c])
    for c in late:
        zed[c] = z_start(c, row[c])
    grads_end(1, copies_1)
    for c in every:
        gat[c] = ag_start(c, zed[c])
    grads_end(0, copies_0)
    for c in every:
        fw_start(c, *gat[c])
    for c in every:
        for copy in gat[c][1]:
            copy.wait_recv()
    full = total[...]
    scale = STEP_SIZE / jnp.sqrt(jnp.sum(full * full, keepdims=True) / full.size + EPSILON)
    for m in range(probe.shape[1]):
        for part in range(2):
            new_ref[part, m] = (
                probe[part, m] - scale * total[pl.ds((2 * m + part) * win, win)]
            )
    for copy in halo_0 + halo_1 + copies_0 + copies_1:
        copy.wait_send()
    for c in every:
        for copy in [pair[c]] + row[c] + zed[c] + gat[c][0] + gat[c][1]:
            copy.wait_send()


def out_kernel(grad, new, grad_out, new_out, sem):
    copies = []
    for part in range(2):
        for lay in range(grad.shape[1]):
            copies.append((grad.at[part, lay], grad_out.at[part, lay]))
        copies.append((new.at[part], new_out.at[part]))
    copies = [
        pltpu.make_async_copy(src, dst, sem.at[i]) for i, (src, dst) in enumerate(copies)
    ]
    for copy in copies:
        copy.start()
    for copy in copies:
        copy.wait()


def on_device(object_tiles, probe_modes, offsets, amplitude):
    n_row, n_col = lax.axis_size("row"), lax.axis_size("col")
    n_z = n_col // 2
    tile, win, scans = object_tiles.shape[2], probe_modes.shape[2], offsets.shape[2]
    tall, nt = tile + 2 * HALO, tile // LANES
    modes = probe_modes.shape[1]
    g_rows = 2 * modes * win
    size = g_rows // CHUNKS
    chunks = tuple((i * size, size) for i in range(CHUNKS))
    piece = g_rows // 2 // n_row
    vmem = pl.BlockSpec(memory_space=pltpu.VMEM)
    smem = pl.BlockSpec(memory_space=pltpu.SMEM)
    hbm = pl.BlockSpec(memory_space=pltpu.HBM)
    dma = pltpu.SemaphoreType.DMA
    block = lambda *shape: pltpu.VMEM(shape, F32)
    pairs = offsets.transpose(0, 1, 3, 2)
    table = jnp.asarray(tables(win))
    grad, new = pl.pallas_call(
        functools.partial(fused_kernel, (n_row, n_col, win, scans, chunks)),
        out_shape=(
            jax.ShapeDtypeStruct(object_tiles.shape, F32),
            jax.ShapeDtypeStruct(probe_modes.shape, F32),
        ),
        in_specs=[smem] + [hbm] * 4,
        out_specs=(vmem, vmem),
        scratch_shapes=[
            block(2, nt + 1, tall, LANES),
            block(2, nt + 1, tall, LANES),
            block(*probe_modes.shape),
            block(*amplitude.shape),
            pltpu.VMEM(table.shape, BF16),
            block(scans, 4, win, win),
            block(scans, 2, 2 * win, 2 * win),
            block(scans, 2, 2 * win, 2 * win),
            block(scans, win, win),
            block(2, 2, scans, win, win),
            block(g_rows, win),
            block(scans, 2, nt + 1, 2 * tall - win, LANES),
            block(2, 2, nt + 1, tall, LANES),
            block(2, tile // 2, LANES),
            block(2, tile // 2, LANES),
            block(2, tall // 2, LANES),
            block(2, tall // 2, LANES),
            block(2, 2, nt, HALO, LANES),
            block(2, 2, nt, HALO, LANES),
            block(2, tall // 2, LANES),
            block(2, tall // 2, LANES),
            block(2, tall // 2, LANES),
            block(2, tall // 2, LANES),
            block(g_rows // 2, win),
            block(g_rows // 2, win),
            block(n_row - 1, piece, win),
            block(n_z, piece, win),
            block(g_rows, win),
            dma((4 * nt + 3,)),
            dma((2, 8)),
            dma((2, 8)),
            dma((2, 8)),
            dma((2, 8)),
            dma((CHUNKS,)),
            dma((CHUNKS,)),
            dma((CHUNKS, n_row - 1)),
            dma((CHUNKS, n_row - 1)),
            dma((CHUNKS, n_z - 1)),
            dma((CHUNKS, n_z - 1)),
            dma((CHUNKS, n_row - 1)),
            dma((CHUNKS, n_row - 1)),
            dma((CHUNKS, n_row)),
            dma((CHUNKS, n_row)),
        ],
        compiler_params=pltpu.CompilerParams(
            collective_id=0, has_side_effects=True, vmem_limit_bytes=48 * 1024 * 1024
        ),
    )(pairs, object_tiles, probe_modes, amplitude, table)
    return pl.pallas_call(
        out_kernel,
        out_shape=(
            jax.ShapeDtypeStruct(object_tiles.shape, F32),
            jax.ShapeDtypeStruct(probe_modes.shape, F32),
        ),
        in_specs=[vmem, vmem],
        out_specs=(hbm, hbm),
        scratch_shapes=[dma((6,))],
    )(grad, new)


CHUNKS = 2


def solution(mesh):
    placed = (
        P(None, None, "row", "col"),
        P(),
        P("row", "col", None, None),
        P("row", "col", None, None, None),
    )
    return jax.shard_map(
        on_device,
        mesh=mesh,
        in_specs=placed,
        out_specs=(P(None, None, "row", "col"), P()),
        check_vma=False,
    )
```

```python
import functools

import jax
import jax.numpy as jnp
import numpy as np
from jax import lax
from jax.experimental import pallas as pl
from jax.experimental.pallas import tpu as pltpu
from jax.sharding import PartitionSpec as P

HALO = 32
PROP = 0.002
SHIFT_AMP = 0.5
STEP_SIZE = 0.5
EPSILON = 1e-06
LANES = 128
SUB = 8
MESH = pl.DeviceIdType.MESH
F32 = jnp.float32
BF16 = jnp.bfloat16


def tables(win):
    k = np.arange(win)
    c = np.exp(-2j * np.pi * (k[:, None] * k[None, :] % win) / win) / np.sqrt(win)
    freq = (k + win // 2) % win - win // 2
    kern = np.conj(c) @ np.diag(np.exp(-1j * PROP * freq**2)) @ c
    out = []
    for m in (c, np.conj(c), kern, np.conj(kern)):
        full = np.block([[m.real, m.imag], [-m.imag, m.real]])
        high = full.astype(np.float32).astype(jnp.bfloat16)
        low = (full - high.astype(np.float64)).astype(np.float32).astype(jnp.bfloat16)
        out += [high, low]
    return np.stack(out)


FWD, INV, KER, KER_INV = 0, 1, 2, 3


def split(x):
    high = x.astype(BF16)
    return high, (x - high.astype(F32)).astype(BF16)


def dot(a, b):
    return jnp.dot(a, b, preferred_element_type=F32)


def right(x, tab, which):
    high, low = split(x)
    return dot(high, tab[2 * which]) + (
        dot(low, tab[2 * which]) + dot(high, tab[2 * which + 1])
    )


def left(x, tab, which):
    high, low = split(x)
    which = which ^ 1
    return dot(tab[2 * which], high) + (
        dot(tab[2 * which], low) + dot(tab[2 * which + 1], high)
    )


def swap(y):
    w = y.shape[0] // 2
    top = jnp.concatenate([y[:w, :w], y[w:, :w]], axis=1)
    low = jnp.concatenate([y[:w, w:], y[w:, w:]], axis=1)
    return jnp.concatenate([top, low], axis=0)


def twice(x, axis):
    return jnp.concatenate([x, x], axis=axis)


def lane(rows):
    return lax.broadcasted_iota(jnp.int32, (rows, LANES), 1)


FOLD = HALO // 2


def fold(get, rows, first):
    at = lane(rows // 2)
    out = None
    for part in range(2):
        x = get(part)
        for h in range(2):
            low = HALO * (2 * h + part)
            block = jnp.concatenate(
                [x[HALO * b + FOLD * h : HALO * b + FOLD * (h + 1)] for b in range(rows // HALO)],
                axis=0,
            )
            shift = (low - first) % LANES
            block = pltpu.roll(block, shift, 1) if shift else block
            keep = (at >= low) & (at < low + HALO)
            out = jnp.where(keep, block, 0.0 if out is None else out)
    return out


def unfold(x, part, first):
    halves = []
    for h in range(2):
        shift = (first - HALO * (2 * h + part)) % LANES
        halves.append(pltpu.roll(x, shift, 1) if shift else x)
    return jnp.concatenate(
        [
            halves[h][FOLD * b : FOLD * (b + 1)]
            for b in range(x.shape[0] // FOLD)
            for h in range(2)
        ],
        axis=0,
    )


def remote(src, dst, ssem, rsem, to):
    copy = pltpu.make_async_remote_copy(
        src_ref=src,
        dst_ref=dst,
        send_sem=ssem,
        recv_sem=rsem,
        device_id=to,
        device_id_type=MESH,
    )
    copy.start()
    return copy


def fused_kernel(
    sizes,
    off_hbm,
    obj_hbm,
    probe_hbm,
    amp_hbm,
    tab_hbm,
    grad_ref,
    new_ref,
    off_ref,
    ext_0,
    ext_1,
    probe,
    amp,
    tab,
    winds,
    wave,
    far,
    factor,
    gobj,
    gprobe,
    zpad,
    acc,
    pack_l,
    pack_r,
    halo_l,
    halo_r,
    from_top,
    from_bot,
    edge_l,
    edge_r,
    from_l,
    from_r,
    half_in,
    half_sum,
    r_parts,
    z_parts,
    total,
    in_sem,
    h_send,
    h_recv,
    g_send,
    g_recv,
    pair_send,
    pair_recv,
    r_send,
    r_recv,
    z_send,
    z_recv,
    ag_send,
    ag_recv,
    fw_send,
    fw_recv,
):
    n_row, n_col, win, scans, chunks = sizes
    n_z = n_col // 2
    ext = (ext_0, ext_1)
    tile = grad_ref.shape[2]
    tall = tile + 2 * HALO
    nt = tile // LANES
    pad = tall - win
    my_r, my_c = lax.axis_index("row"), lax.axis_index("col")

    def at(dr, dc):
        return lax.rem(my_r + dr % n_row, n_row), lax.rem(my_c + dc % n_col, n_col)

    barrier = pltpu.get_barrier_semaphore()
    mates = {(dr % n_row, dc % n_col) for dr in (-1, 0, 1) for dc in (-1, 0, 1)}
    mates |= {(k, 0) for k in range(n_row)} | {(0, 2 * k) for k in range(n_z)}
    mates.discard((0, 0))
    for mate in sorted(mates):
        pl.semaphore_signal(barrier, inc=1, device_id=at(*mate), device_id_type=MESH)
    loads = []
    for lay in range(2):
        for part in range(2):
            for t in range(nt):
                loads.append(
                    pltpu.make_async_copy(
                        obj_hbm.at[part, lay, :, pl.ds(t * LANES, LANES)],
                        ext[lay].at[part, t, pl.ds(HALO, tile), :],
                        in_sem.at[len(loads)],
                    )
                )
    per_lay = len(loads) // 2
    for src, dst in ((off_hbm, off_ref), (probe_hbm, probe), (tab_hbm, tab), (amp_hbm, amp)):
        loads.append(pltpu.make_async_copy(src, dst, in_sem.at[len(loads)]))
    for load in loads:
        load.start()

    head, tail = pl.ds(0, FOLD), pl.ds((tile - HALO) // 2, FOLD)
    mid, after = pl.ds(FOLD, tile // 2), pl.ds(FOLD + tile // 2, FOLD)

    def pack(lay):
        for load in loads[lay * per_lay : (lay + 1) * per_lay]:
            load.wait()
        own = pl.ds(HALO, tile)
        pack_l[lay] = fold(lambda part: ext[lay][part, 0, own, :], tile, 0)
        pack_r[lay] = fold(lambda part: ext[lay][part, nt - 1, own, :], tile, LANES - HALO)

    def halo_start(lay):
        e, left_in, right_in = ext[lay], halo_l.at[lay], halo_r.at[lay]
        pl_, pr_ = pack_l.at[lay], pack_r.at[lay]
        own = pl.ds(0, nt)
        plan = [
            (e.at[:, own, pl.ds(tile, HALO)], e.at[:, own, pl.ds(0, HALO)], (1, 0)),
            (e.at[:, own, pl.ds(HALO, HALO)], e.at[:, own, pl.ds(HALO + tile, HALO)], (-1, 0)),
            (pr_, left_in.at[mid], (0, 1)),
            (pl_, right_in.at[mid], (0, -1)),
            (pr_.at[tail], left_in.at[head], (1, 1)),
            (pr_.at[head], left_in.at[after], (-1, 1)),
            (pl_.at[tail], right_in.at[head], (1, -1)),
            (pl_.at[head], right_in.at[after], (-1, -1)),
        ]
        return [
            remote(src, dst, h_send.at[lay, i], h_recv.at[lay, i], at(*to))
            for i, (src, dst, to) in enumerate(plan)
        ]

    def halo_end(lay, copies):
        for copy in copies:
            copy.wait_recv()
        for part in range(2):
            near = unfold(halo_r[lay], part, 0)
            distant = unfold(halo_l[lay], part, LANES - HALO)
            x = lane(tall)
            ext[lay][part, nt, pl.ds(0, tall), :] = jnp.where(
                x < HALO, near, jnp.where(x >= LANES - HALO, distant, 0.0)
            )

    def spot(s):
        row = off_ref[0, 0, 0, s]
        col = off_ref[0, 0, 1, s] - HALO
        col = jnp.where(col < 0, col + (nt + 1) * LANES, col)
        first = lax.div(col, LANES)
        second = jnp.where(first == nt, 0, first + 1)
        return row, first, second, col - first * LANES

    def windows(lay):
        @pl.loop(0, scans)
        def _(s):
            row, first, second, rem = spot(s)
            for part in range(2):
                a = ext[lay][part, first, pl.ds(row, win), :]
                b = ext[lay][part, second, pl.ds(row, win), :]
                block = jnp.where(lane(win) >= rem, a, b)
                winds[s, 2 * part + lay] = pltpu.roll(block, lax.rem(LANES - rem, LANES), 1)

    pack(0)
    pl.semaphore_wait(barrier, len(mates))
    halo_0 = halo_start(0)
    pack(1)
    halo_1 = halo_start(1)
    gprobe[...] = jnp.zeros_like(gprobe)
    gobj[...] = jnp.zeros_like(gobj)
    zpad[...] = jnp.zeros_like(zpad)
    for load in loads[2 * per_lay :]:
        load.wait()
    halo_end(0, halo_0)
    windows(0)

    for s in range(scans):
        or_, oi_ = winds[s, 0], winds[s, 2]
        for p in range(2):
            rows = []
            for m in range(2):
                pr, pi = probe[0, 2 * p + m], probe[1, 2 * p + m]
                rows.append(
                    jnp.concatenate([pr * or_ - pi * oi_, pr * oi_ + pi * or_], axis=1)
                )
            psi = jnp.concatenate(rows, axis=0)
            wave[s, p] = left(swap(right(psi, tab, KER)), tab, KER)

    halo_end(1, halo_1)
    windows(1)

    for s in range(scans):
        power = None
        for p in range(2):
            w = wave[s, p]
            wr, wi = w[:win], w[win:]
            o1r, o1i = twice(winds[s, 1], 1), twice(winds[s, 3], 1)
            psi = jnp.concatenate([wr * o1r - wi * o1i, wr * o1i + wi * o1r], axis=0)
            psi = right(swap(left(psi, tab, FWD)), tab, FWD)
            far[s, p] = psi
            sq = psi * psi
            part_sum = (sq[:win, :win] + sq[:win, win:]) + (sq[win:, :win] + sq[win:, win:])
            power = part_sum if power is None else power + part_sum
        root = jnp.sqrt(power + SHIFT_AMP)
        factor[s] = 2.0 * (root - amp[0, 0, s]) / root

    def first_half(p, s):
        g = far[s, p] * twice(twice(factor[s], 0), 1)
        g = left(swap(right(g, tab, INV)), tab, INV)
        w = wave[s, p]
        gr, gi, wr, wi = g[:win], g[win:], w[:win], w[win:]
        re = wr * gr + wi * gi
        im = wr * gi - wi * gr
        gobj[1, 0, s] += re[:, :win] + re[:, win:]
        gobj[1, 1, s] += im[:, :win] + im[:, win:]
        o1r, o1i = twice(winds[s, 1], 1), twice(winds[s, 3], 1)
        far[s, p] = jnp.concatenate([o1r * gr + o1i * gi, o1r * gi - o1i * gr], axis=0)

    def second_half(p, s):
        g = right(swap(left(far[s, p], tab, KER_INV)), tab, KER_INV)
        o0r, o0i = winds[s, 0], winds[s, 2]
        re = im = None
        for m in range(2):
            gr, gi = g[m * win : (m + 1) * win, :win], g[m * win : (m + 1) * win, win:]
            pr, pi = probe[0, 2 * p + m], probe[1, 2 * p + m]
            a = pr * gr + pi * gi
            b = pr * gi - pi * gr
            re, im = (a, b) if re is None else (re + a, im + b)
            base = (2 * p + m) * 2 * win
            gprobe[pl.ds(base, win)] += o0r * gr + o0i * gi
            gprobe[pl.ds(base + win, win)] += o0r * gi - o0i * gr
        gobj[0, 0, s] += re
        gobj[0, 1, s] += im

    def place(lay):
        starts = []
        for s in range(scans):
            row, first, second, rem = spot(s)
            starts.append(pad - row)
            where = jnp.where(lane(win) >= rem, first, second)
            for part in range(2):
                block = pltpu.roll(gobj[lay, part, s], rem, 1)
                for t in range(nt + 1):
                    zpad[s, part, t, pl.ds(pad, win), :] = jnp.where(where == t, block, 0.0)
        for part in range(2):
            for t in range(nt + 1):
                value = None
                for s in range(scans):
                    block = zpad[s, part, t, pl.ds(starts[s], tall), :]
                    value = block if value is None else value + block
                acc[lay, part, t] = value

    def grads_start(lay):
        a, er, el = acc.at[lay], edge_r.at[lay], edge_l.at[lay]
        fl, fr = from_l.at[lay], from_r.at[lay]
        edge_r[lay] = fold(lambda part: acc[lay, part, nt], tall, 0)
        edge_l[lay] = fold(lambda part: acc[lay, part, nt], tall, LANES - HALO)
        own = pl.ds(0, nt)
        plan = [
            (a.at[:, own, pl.ds(0, HALO)], from_bot.at[lay], (-1, 0)),
            (a.at[:, own, pl.ds(HALO + tile, HALO)], from_top.at[lay], (1, 0)),
            (er.at[mid], fl.at[mid], (0, 1)),
            (el.at[mid], fr.at[mid], (0, -1)),
            (er.at[head], fl.at[after], (-1, 1)),
            (er.at[after], fl.at[head], (1, 1)),
            (el.at[head], fr.at[after], (-1, -1)),
            (el.at[after], fr.at[head], (1, -1)),
        ]
        return [
            remote(src, dst, g_send.at[lay, i], g_recv.at[lay, i], at(*to))
            for i, (src, dst, to) in enumerate(plan)
        ]

    def grads_end(lay, copies):
        for copy in copies:
            copy.wait_recv()
        x = lane(tall)
        for part in range(2):
            for t in range(nt):
                value = acc[lay, part, t, pl.ds(HALO, tile), :]
                top, bot = from_top[lay, part, t], from_bot[lay, part, t]
                for ref, first, edge in ((from_l, 0, 0), (from_r, LANES - HALO, nt - 1)):
                    if t == edge:
                        block = unfold(ref[lay], part, first)
                        block = jnp.where((x >= first) & (x < first + HALO), block, 0.0)
                        value = value + block[HALO : HALO + tile]
                        top = top + block[:HALO]
                        bot = bot + block[HALO + tile :]
                cols = pl.ds(t * LANES, LANES)
                grad_ref[part, lay, pl.ds(0, HALO), cols] = value[:HALO] + top
                grad_ref[part, lay, pl.ds(HALO, tile - 2 * HALO), cols] = value[HALO:-HALO]
                grad_ref[part, lay, pl.ds(tile - HALO, HALO), cols] = value[-HALO:] + bot

    odd = lax.rem(my_c, 2)
    partner = (my_r, my_c + 1 - 2 * odd)
    my_z = lax.div(my_c, 2)

    def span(c):
        start, size = chunks[c]
        half = size // 2
        piece = half // n_row
        return start, half, piece, start // 2, start // 2 // n_row

    def rows_at(start, size):
        return pl.ds(pl.multiple_of(start, SUB), size)

    def row_mate(k):
        return lax.rem(my_r + k, n_row)

    def pair_start(c):
        start, half, piece, hs, ps = span(c)
        return remote(
            gprobe.at[rows_at(start + (1 - odd) * half, half)],
            half_in.at[pl.ds(hs, half)],
            pair_send.at[c],
            pair_recv.at[c],
            partner,
        )

    def r_start(c, pair):
        start, half, piece, hs, ps = span(c)
        pair.wait_recv()
        half_sum[pl.ds(hs, half)] = (
            gprobe[rows_at(start + odd * half, half)] + half_in[pl.ds(hs, half)]
        )
        copies = []
        for k in range(1, n_row):
            q = row_mate(k)
            copies.append(
                remote(
                    half_sum.at[rows_at(hs + q * piece, piece)],
                    r_parts.at[k - 1, pl.ds(ps, piece)],
                    r_send.at[c, k - 1],
                    r_recv.at[c, k - 1],
                    (q, my_c),
                )
            )
        return copies

    def z_start(c, before):
        start, half, piece, hs, ps = span(c)
        for copy in before:
            copy.wait_recv()
        value = half_sum[rows_at(hs + my_r * piece, piece)]
        for k in range(n_row - 1):
            value = value + r_parts[k, pl.ds(ps, piece)]
        z_parts[my_z, pl.ds(ps, piece)] = value
        mine = z_parts.at[my_z, pl.ds(ps, piece)]
        return [
            remote(mine, mine, z_send.at[c, k - 1], z_recv.at[c, k - 1], at(0, 2 * k))
            for k in range(1, n_z)
        ]

    def ag_start(c, before):
        start, half, piece, hs, ps = span(c)
        for copy in before:
            copy.wait_recv()
        value = z_parts[0, pl.ds(ps, piece)]
        for k in range(1, n_z):
            value = value + z_parts[k, pl.ds(ps, piece)]
        own = rows_at(start + odd * half + my_r * piece, piece)
        total[own] = value
        mine = total.at[own]
        copies = [
            remote(mine, mine, ag_send.at[c, k - 1], ag_recv.at[c, k - 1], at(k, 0))
            for k in range(1, n_row)
        ]
        return copies, [remote(mine, mine, fw_send.at[c, 0], fw_recv.at[c, 0], partner)]

    def fw_start(c, copies, forwards):
        start, half, piece, hs, ps = span(c)
        for k in range(1, n_row):
            copies[k - 1].wait_recv()
            q = lax.rem(my_r + n_row - k, n_row)
            got = total.at[rows_at(start + odd * half + q * piece, piece)]
            forwards.append(remote(got, got, fw_send.at[c, k], fw_recv.at[c, k], partner))

    for s in range(scans):
        first_half(0, s)
    for s in range(scans):
        second_half(0, s)

    early, late = range(len(chunks) // 2), range(len(chunks) // 2, len(chunks))
    every = range(len(chunks))
    pair, row, zed, gat = {}, {}, {}, {}
    for c in early:
        pair[c] = pair_start(c)

    for s in range(scans):
        first_half(1, s)

    for c in early:
        row[c] = r_start(c, pair[c])
    place(1)
    copies_1 = grads_start(1)

    for s in range(scans):
        second_half(1, s)

    for c in late:
        pair[c] = pair_start(c)
    place(0)
    for c in late:
        row[c] = r_start(c, pair[c])
    copies_0 = grads_start(0)
    for c in early:
        zed[c] = z_start(c, row[c])
    for c in late:
        zed[c] = z_start(c, row[c])
    grads_end(1, copies_1)
    for c in every:
        gat[c] = ag_start(c, zed[c])
    grads_end(0, copies_0)
    for c in every:
        fw_start(c, *gat[c])
    for c in every:
        for copy in gat[c][1]:
            copy.wait_recv()
    full = total[...]
    scale = STEP_SIZE / jnp.sqrt(jnp.sum(full * full, keepdims=True) / full.size + EPSILON)
    for m in range(probe.shape[1]):
        for part in range(2):
            new_ref[part, m] = (
                probe[part, m] - scale * total[pl.ds((2 * m + part) * win, win)]
            )
    for copy in halo_0 + halo_1 + copies_0 + copies_1:
        copy.wait_send()
    for c in every:
        for copy in [pair[c]] + row[c] + zed[c] + gat[c][0] + gat[c][1]:
            copy.wait_send()


def out_kernel(grad, new, grad_out, new_out, sem):
    copies = []
    for part in range(2):
        for lay in range(grad.shape[1]):
            copies.append((grad.at[part, lay], grad_out.at[part, lay]))
        copies.append((new.at[part], new_out.at[part]))
    copies = [
        pltpu.make_async_copy(src, dst, sem.at[i]) for i, (src, dst) in enumerate(copies)
    ]
    for copy in copies:
        copy.start()
    for copy in copies:
        copy.wait()


def on_device(object_tiles, probe_modes, offsets, amplitude):
    n_row, n_col = lax.axis_size("row"), lax.axis_size("col")
    n_z = n_col // 2
    tile, win, scans = object_tiles.shape[2], probe_modes.shape[2], offsets.shape[2]
    tall, nt = tile + 2 * HALO, tile // LANES
    modes = probe_modes.shape[1]
    g_rows = 2 * modes * win
    size = g_rows // CHUNKS
    chunks = tuple((i * size, size) for i in range(CHUNKS))
    piece = g_rows // 2 // n_row
    vmem = pl.BlockSpec(memory_space=pltpu.VMEM)
    hbm = pl.BlockSpec(memory_space=pltpu.HBM)
    dma = pltpu.SemaphoreType.DMA
    block = lambda *shape: pltpu.VMEM(shape, F32)
    pairs = offsets.transpose(0, 1, 3, 2)
    table = jnp.asarray(tables(win))
    grad, new = pl.pallas_call(
        functools.partial(fused_kernel, (n_row, n_col, win, scans, chunks)),
        out_shape=(
            jax.ShapeDtypeStruct(object_tiles.shape, F32),
            jax.ShapeDtypeStruct(probe_modes.shape, F32),
        ),
        in_specs=[hbm] * 5,
        out_specs=(vmem, vmem),
        scratch_shapes=[
            pltpu.SMEM(pairs.shape, jnp.int32),
            block(2, nt + 1, tall, LANES),
            block(2, nt + 1, tall, LANES),
            block(*probe_modes.shape),
            block(*amplitude.shape),
            pltpu.VMEM(table.shape, BF16),
            block(scans, 4, win, win),
            block(scans, 2, 2 * win, 2 * win),
            block(scans, 2, 2 * win, 2 * win),
            block(scans, win, win),
            block(2, 2, scans, win, win),
            block(g_rows, win),
            block(scans, 2, nt + 1, 2 * tall - win, LANES),
            block(2, 2, nt + 1, tall, LANES),
            block(2, tile // 2, LANES),
            block(2, tile // 2, LANES),
            block(2, tall // 2, LANES),
            block(2, tall // 2, LANES),
            block(2, 2, nt, HALO, LANES),
            block(2, 2, nt, HALO, LANES),
            block(2, tall // 2, LANES),
            block(2, tall // 2, LANES),
            block(2, tall // 2, LANES),
            block(2, tall // 2, LANES),
            block(g_rows // 2, win),
            block(g_rows // 2, win),
            block(n_row - 1, piece, win),
            block(n_z, piece, win),
            block(g_rows, win),
            dma((4 * nt + 4,)),
            dma((2, 8)),
            dma((2, 8)),
            dma((2, 8)),
            dma((2, 8)),
            dma((CHUNKS,)),
            dma((CHUNKS,)),
            dma((CHUNKS, n_row - 1)),
            dma((CHUNKS, n_row - 1)),
            dma((CHUNKS, n_z - 1)),
            dma((CHUNKS, n_z - 1)),
            dma((CHUNKS, n_row - 1)),
            dma((CHUNKS, n_row - 1)),
            dma((CHUNKS, n_row)),
            dma((CHUNKS, n_row)),
        ],
        compiler_params=pltpu.CompilerParams(
            collective_id=0, has_side_effects=True, vmem_limit_bytes=48 * 1024 * 1024
        ),
    )(
        *[
            pltpu.with_memory_space_constraint(x, pltpu.HBM)
            for x in (pairs, object_tiles, probe_modes, amplitude, table)
        ],
    )
    return pl.pallas_call(
        out_kernel,
        out_shape=(
            jax.ShapeDtypeStruct(object_tiles.shape, F32),
            jax.ShapeDtypeStruct(probe_modes.shape, F32),
        ),
        in_specs=[vmem, vmem],
        out_specs=(hbm, hbm),
        scratch_shapes=[dma((6,))],
        compiler_params=pltpu.CompilerParams(vmem_limit_bytes=1024 * 1024),
    )(grad, new)


CHUNKS = 2


def solution(mesh):
    placed = (
        P(None, None, "row", "col"),
        P(),
        P("row", "col", None, None),
        P("row", "col", None, None, None),
    )
    return jax.shard_map(
        on_device,
        mesh=mesh,
        in_specs=placed,
        out_specs=(P(None, None, "row", "col"), P()),
        check_vma=False,
    )
```

```python
import functools

import jax
import jax.numpy as jnp
import numpy as np
from jax import lax
from jax.experimental import pallas as pl
from jax.experimental.pallas import tpu as pltpu
from jax.sharding import PartitionSpec as P

HALO = 32
PROP = 0.002
SHIFT_AMP = 0.5
STEP_SIZE = 0.5
EPSILON = 1e-06
LANES = 128
SUB = 8
MESH = pl.DeviceIdType.MESH
F32 = jnp.float32
BF16 = jnp.bfloat16


def tables(win):
    k = np.arange(win)
    c = np.exp(-2j * np.pi * (k[:, None] * k[None, :] % win) / win) / np.sqrt(win)
    freq = (k + win // 2) % win - win // 2
    kern = np.conj(c) @ np.diag(np.exp(-1j * PROP * freq**2)) @ c
    out = []
    for m in (c, np.conj(c), kern, np.conj(kern)):
        full = np.block([[m.real, m.imag], [-m.imag, m.real]])
        high = full.astype(np.float32).astype(jnp.bfloat16)
        low = (full - high.astype(np.float64)).astype(np.float32).astype(jnp.bfloat16)
        out += [high, low]
    return np.stack(out)


FWD, INV, KER, KER_INV = 0, 1, 2, 3


def split(x):
    high = x.astype(BF16)
    return high, (x - high.astype(F32)).astype(BF16)


def dot(a, b):
    return jnp.dot(a, b, preferred_element_type=F32)


def right(x, tab, which):
    high, low = split(x)
    return dot(high, tab[2 * which]) + (
        dot(low, tab[2 * which]) + dot(high, tab[2 * which + 1])
    )


def left(x, tab, which):
    high, low = split(x)
    which = which ^ 1
    return dot(tab[2 * which], high) + (
        dot(tab[2 * which], low) + dot(tab[2 * which + 1], high)
    )


def swap(y):
    w = y.shape[0] // 2
    top = jnp.concatenate([y[:w, :w], y[w:, :w]], axis=1)
    low = jnp.concatenate([y[:w, w:], y[w:, w:]], axis=1)
    return jnp.concatenate([top, low], axis=0)


def twice(x, axis):
    return jnp.concatenate([x, x], axis=axis)


def lane(rows):
    return lax.broadcasted_iota(jnp.int32, (rows, LANES), 1)


FOLD = HALO // 2


def fold(get, rows, first):
    at = lane(rows // 2)
    out = None
    for part in range(2):
        x = get(part)
        for h in range(2):
            low = HALO * (2 * h + part)
            block = jnp.concatenate(
                [x[HALO * b + FOLD * h : HALO * b + FOLD * (h + 1)] for b in range(rows // HALO)],
                axis=0,
            )
            shift = (low - first) % LANES
            block = pltpu.roll(block, shift, 1) if shift else block
            keep = (at >= low) & (at < low + HALO)
            out = jnp.where(keep, block, 0.0 if out is None else out)
    return out


def unfold(x, part, first):
    halves = []
    for h in range(2):
        shift = (first - HALO * (2 * h + part)) % LANES
        halves.append(pltpu.roll(x, shift, 1) if shift else x)
    return jnp.concatenate(
        [
            halves[h][FOLD * b : FOLD * (b + 1)]
            for b in range(x.shape[0] // FOLD)
            for h in range(2)
        ],
        axis=0,
    )


def remote(src, dst, ssem, rsem, to):
    copy = pltpu.make_async_remote_copy(
        src_ref=src,
        dst_ref=dst,
        send_sem=ssem,
        recv_sem=rsem,
        device_id=to,
        device_id_type=MESH,
    )
    copy.start()
    return copy


def fused_kernel(
    sizes,
    off_hbm,
    obj_hbm,
    probe_hbm,
    amp_hbm,
    tab_hbm,
    grad_ref,
    new_ref,
    off_ref,
    ext_0,
    ext_1,
    probe,
    amp,
    tab,
    winds,
    wave,
    far,
    factor,
    gobj,
    gprobe,
    zpad,
    acc,
    pack_l,
    pack_r,
    halo_l,
    halo_r,
    from_top,
    from_bot,
    edge_l,
    edge_r,
    from_l,
    from_r,
    half_in,
    half_sum,
    r_parts,
    z_parts,
    total,
    in_sem,
    h_send,
    h_recv,
    g_send,
    g_recv,
    pair_send,
    pair_recv,
    r_send,
    r_recv,
    z_send,
    z_recv,
    ag_send,
    ag_recv,
    fw_send,
    fw_recv,
):
    n_row, n_col, win, scans, chunks = sizes
    n_z = n_col // 2
    ext = (ext_0, ext_1)
    tile = grad_ref.shape[2]
    tall = tile + 2 * HALO
    nt = tile // LANES
    pad = tall - win
    my_r, my_c = lax.axis_index("row"), lax.axis_index("col")

    def at(dr, dc):
        return lax.rem(my_r + dr % n_row, n_row), lax.rem(my_c + dc % n_col, n_col)

    barrier = pltpu.get_barrier_semaphore()
    mates = {(dr % n_row, dc % n_col) for dr in (-1, 0, 1) for dc in (-1, 0, 1)}
    mates |= {(k, 0) for k in range(n_row)} | {(0, 2 * k) for k in range(n_z)}
    mates.discard((0, 0))
    for mate in sorted(mates):
        pl.semaphore_signal(barrier, inc=1, device_id=at(*mate), device_id_type=MESH)
    loads = []
    for lay in range(2):
        for part in range(2):
            for t in range(nt):
                loads.append(
                    pltpu.make_async_copy(
                        obj_hbm.at[part, lay, :, pl.ds(t * LANES, LANES)],
                        ext[lay].at[part, t, pl.ds(HALO, tile), :],
                        in_sem.at[len(loads)],
                    )
                )
    per_lay = len(loads) // 2
    for src, dst in ((off_hbm, off_ref), (probe_hbm, probe), (tab_hbm, tab), (amp_hbm, amp)):
        loads.append(pltpu.make_async_copy(src, dst, in_sem.at[len(loads)]))
    for load in loads:
        load.start()

    head, tail = pl.ds(0, FOLD), pl.ds((tile - HALO) // 2, FOLD)
    mid, after = pl.ds(FOLD, tile // 2), pl.ds(FOLD + tile // 2, FOLD)

    def pack(lay):
        for load in loads[lay * per_lay : (lay + 1) * per_lay]:
            load.wait()
        own = pl.ds(HALO, tile)
        pack_l[lay] = fold(lambda part: ext[lay][part, 0, own, :], tile, 0)
        pack_r[lay] = fold(lambda part: ext[lay][part, nt - 1, own, :], tile, LANES - HALO)

    def halo_start(lay, which):
        e, left_in, right_in = ext[lay], halo_l.at[lay], halo_r.at[lay]
        pl_, pr_ = pack_l.at[lay], pack_r.at[lay]
        own = pl.ds(0, nt)
        plan = [
            (e.at[:, own, pl.ds(tile, HALO)], e.at[:, own, pl.ds(0, HALO)], (1, 0)),
            (e.at[:, own, pl.ds(HALO, HALO)], e.at[:, own, pl.ds(HALO + tile, HALO)], (-1, 0)),
            (pr_, left_in.at[mid], (0, 1)),
            (pl_, right_in.at[mid], (0, -1)),
            (pr_.at[tail], left_in.at[head], (1, 1)),
            (pr_.at[head], left_in.at[after], (-1, 1)),
            (pl_.at[tail], right_in.at[head], (1, -1)),
            (pl_.at[head], right_in.at[after], (-1, -1)),
        ]
        return [
            remote(src, dst, h_send.at[lay, i], h_recv.at[lay, i], at(*to))
            for i, (src, dst, to) in ((i, plan[i]) for i in which)
        ]

    def halo_end(lay, copies, rows):
        for copy in copies:
            copy.wait_recv()
        for part in range(2):
            near = unfold(halo_r[lay], part, 0)
            distant = unfold(halo_l[lay], part, LANES - HALO)
            x = lane(tall)
            ext[lay][part, nt, pl.ds(0, tall), :] = jnp.where(
                x < HALO, near, jnp.where(x >= LANES - HALO, distant, 0.0)
            )
        for copy in rows:
            copy.wait_recv()

    def spot(s):
        row = off_ref[0, 0, 0, s]
        col = off_ref[0, 0, 1, s] - HALO
        col = jnp.where(col < 0, col + (nt + 1) * LANES, col)
        first = lax.div(col, LANES)
        second = jnp.where(first == nt, 0, first + 1)
        return row, first, second, col - first * LANES

    def windows(lay):
        for s in range(scans):
            row, first, second, rem = spot(s)
            for part in range(2):
                a = ext[lay][part, first, pl.ds(row, win), :]
                b = ext[lay][part, second, pl.ds(row, win), :]
                block = jnp.where(lane(win) >= rem, a, b)
                winds[s, 2 * part + lay] = pltpu.roll(block, lax.rem(LANES - rem, LANES), 1)

    sides, ends = (4, 5, 6, 7, 2, 3), (0, 1)
    pack(0)
    pack(1)
    pl.semaphore_wait(barrier, len(mates))
    sides_0 = halo_start(0, sides)
    sides_1 = halo_start(1, sides)
    ends_0 = halo_start(0, ends)
    ends_1 = halo_start(1, ends)
    gprobe[...] = jnp.zeros_like(gprobe)
    gobj[...] = jnp.zeros_like(gobj)
    zpad[...] = jnp.zeros_like(zpad)
    for load in loads[2 * per_lay :]:
        load.wait()
    halo_end(0, sides_0, ends_0)
    windows(0)

    for s in range(scans):
        or_, oi_ = winds[s, 0], winds[s, 2]
        for p in range(2):
            rows = []
            for m in range(2):
                pr, pi = probe[0, 2 * p + m], probe[1, 2 * p + m]
                rows.append(
                    jnp.concatenate([pr * or_ - pi * oi_, pr * oi_ + pi * or_], axis=1)
                )
            psi = jnp.concatenate(rows, axis=0)
            wave[s, p] = left(swap(right(psi, tab, KER)), tab, KER)

    halo_end(1, sides_1, ends_1)
    windows(1)

    for s in range(scans):
        power = None
        for p in range(2):
            w = wave[s, p]
            wr, wi = w[:win], w[win:]
            o1r, o1i = twice(winds[s, 1], 1), twice(winds[s, 3], 1)
            psi = jnp.concatenate([wr * o1r - wi * o1i, wr * o1i + wi * o1r], axis=0)
            psi = right(swap(left(psi, tab, FWD)), tab, FWD)
            far[s, p] = psi
            sq = psi * psi
            part_sum = (sq[:win, :win] + sq[:win, win:]) + (sq[win:, :win] + sq[win:, win:])
            power = part_sum if power is None else power + part_sum
        root = jnp.sqrt(power + SHIFT_AMP)
        factor[s] = 2.0 * (root - amp[0, 0, s]) / root

    def first_half(p, s):
        g = far[s, p] * twice(twice(factor[s], 0), 1)
        g = left(swap(right(g, tab, INV)), tab, INV)
        w = wave[s, p]
        gr, gi, wr, wi = g[:win], g[win:], w[:win], w[win:]
        re = wr * gr + wi * gi
        im = wr * gi - wi * gr
        gobj[1, 0, s] += re[:, :win] + re[:, win:]
        gobj[1, 1, s] += im[:, :win] + im[:, win:]
        o1r, o1i = twice(winds[s, 1], 1), twice(winds[s, 3], 1)
        far[s, p] = jnp.concatenate([o1r * gr + o1i * gi, o1r * gi - o1i * gr], axis=0)

    def second_half(p, s):
        g = right(swap(left(far[s, p], tab, KER_INV)), tab, KER_INV)
        o0r, o0i = winds[s, 0], winds[s, 2]
        re = im = None
        for m in range(2):
            gr, gi = g[m * win : (m + 1) * win, :win], g[m * win : (m + 1) * win, win:]
            pr, pi = probe[0, 2 * p + m], probe[1, 2 * p + m]
            a = pr * gr + pi * gi
            b = pr * gi - pi * gr
            re, im = (a, b) if re is None else (re + a, im + b)
            base = (2 * p + m) * 2 * win
            gprobe[pl.ds(base, win)] += o0r * gr + o0i * gi
            gprobe[pl.ds(base + win, win)] += o0r * gi - o0i * gr
        gobj[0, 0, s] += re
        gobj[0, 1, s] += im

    def place(lay):
        starts = []
        for s in range(scans):
            row, first, second, rem = spot(s)
            starts.append(pad - row)
            where = jnp.where(lane(win) >= rem, first, second)
            for part in range(2):
                block = pltpu.roll(gobj[lay, part, s], rem, 1)
                for t in range(nt + 1):
                    zpad[s, part, t, pl.ds(pad, win), :] = jnp.where(where == t, block, 0.0)
        for part in range(2):
            for t in range(nt + 1):
                value = None
                for s in range(scans):
                    block = zpad[s, part, t, pl.ds(starts[s], tall), :]
                    value = block if value is None else value + block
                acc[lay, part, t] = value

    def grads_fold(lay):
        edge_r[lay] = fold(lambda part: acc[lay, part, nt], tall, 0)
        edge_l[lay] = fold(lambda part: acc[lay, part, nt], tall, LANES - HALO)

    def grads_start(lay, which):
        a, er, el = acc.at[lay], edge_r.at[lay], edge_l.at[lay]
        fl, fr = from_l.at[lay], from_r.at[lay]
        own = pl.ds(0, nt)
        plan = [
            (a.at[:, own, pl.ds(0, HALO)], from_bot.at[lay], (-1, 0)),
            (a.at[:, own, pl.ds(HALO + tile, HALO)], from_top.at[lay], (1, 0)),
            (er.at[mid], fl.at[mid], (0, 1)),
            (el.at[mid], fr.at[mid], (0, -1)),
            (er.at[head], fl.at[after], (-1, 1)),
            (er.at[after], fl.at[head], (1, 1)),
            (el.at[head], fr.at[after], (-1, -1)),
            (el.at[after], fr.at[head], (1, -1)),
        ]
        return [
            remote(src, dst, g_send.at[lay, i], g_recv.at[lay, i], at(*to))
            for i, (src, dst, to) in ((i, plan[i]) for i in which)
        ]

    def grads_end(lay, copies):
        for copy in copies:
            copy.wait_recv()
        x = lane(tall)
        for part in range(2):
            for t in range(nt):
                value = acc[lay, part, t, pl.ds(HALO, tile), :]
                top, bot = from_top[lay, part, t], from_bot[lay, part, t]
                for ref, first, edge in ((from_l, 0, 0), (from_r, LANES - HALO, nt - 1)):
                    if t == edge:
                        block = unfold(ref[lay], part, first)
                        block = jnp.where((x >= first) & (x < first + HALO), block, 0.0)
                        value = value + block[HALO : HALO + tile]
                        top = top + block[:HALO]
                        bot = bot + block[HALO + tile :]
                cols = pl.ds(t * LANES, LANES)
                grad_ref[part, lay, pl.ds(0, HALO), cols] = value[:HALO] + top
                grad_ref[part, lay, pl.ds(HALO, tile - 2 * HALO), cols] = value[HALO:-HALO]
                grad_ref[part, lay, pl.ds(tile - HALO, HALO), cols] = value[-HALO:] + bot

    odd = lax.rem(my_c, 2)
    partner = (my_r, my_c + 1 - 2 * odd)
    my_z = lax.div(my_c, 2)

    def span(c):
        start, size = chunks[c]
        half = size // 2
        piece = half // n_row
        return start, half, piece, start // 2, start // 2 // n_row

    def rows_at(start, size):
        return pl.ds(pl.multiple_of(start, SUB), size)

    def row_mate(k):
        return lax.rem(my_r + k, n_row)

    def pair_start(c):
        start, half, piece, hs, ps = span(c)
        return remote(
            gprobe.at[rows_at(start + (1 - odd) * half, half)],
            half_in.at[pl.ds(hs, half)],
            pair_send.at[c],
            pair_recv.at[c],
            partner,
        )

    def r_start(c, pair):
        start, half, piece, hs, ps = span(c)
        pair.wait_recv()
        half_sum[pl.ds(hs, half)] = (
            gprobe[rows_at(start + odd * half, half)] + half_in[pl.ds(hs, half)]
        )
        copies = []
        for k in range(1, n_row):
            q = row_mate(k)
            copies.append(
                remote(
                    half_sum.at[rows_at(hs + q * piece, piece)],
                    r_parts.at[k - 1, pl.ds(ps, piece)],
                    r_send.at[c, k - 1],
                    r_recv.at[c, k - 1],
                    (q, my_c),
                )
            )
        return copies

    def z_start(c, before):
        start, half, piece, hs, ps = span(c)
        for copy in before:
            copy.wait_recv()
        value = half_sum[rows_at(hs + my_r * piece, piece)]
        for k in range(n_row - 1):
            value = value + r_parts[k, pl.ds(ps, piece)]
        z_parts[my_z, pl.ds(ps, piece)] = value
        mine = z_parts.at[my_z, pl.ds(ps, piece)]
        return [
            remote(mine, mine, z_send.at[c, k - 1], z_recv.at[c, k - 1], at(0, 2 * k))
            for k in range(1, n_z)
        ]

    def ag_start(c, before):
        start, half, piece, hs, ps = span(c)
        for copy in before:
            copy.wait_recv()
        value = z_parts[0, pl.ds(ps, piece)]
        for k in range(1, n_z):
            value = value + z_parts[k, pl.ds(ps, piece)]
        own = rows_at(start + odd * half + my_r * piece, piece)
        total[own] = value
        mine = total.at[own]
        copies = [
            remote(mine, mine, ag_send.at[c, k - 1], ag_recv.at[c, k - 1], at(k, 0))
            for k in range(1, n_row)
        ]
        return copies, [remote(mine, mine, fw_send.at[c, 0], fw_recv.at[c, 0], partner)]

    def fw_start(c, copies, forwards):
        start, half, piece, hs, ps = span(c)
        for k in range(1, n_row):
            copies[k - 1].wait_recv()
            q = lax.rem(my_r + n_row - k, n_row)
            got = total.at[rows_at(start + odd * half + q * piece, piece)]
            forwards.append(remote(got, got, fw_send.at[c, k], fw_recv.at[c, k], partner))

    early, late = range(len(chunks) // 2), range(len(chunks) // 2, len(chunks))
    every = range(len(chunks))
    pair, row, zed, gat = {}, {}, {}, {}
    for s in range(scans):
        first_half(0, s)
    for s in range(scans):
        second_half(0, s)
    for c in early:
        pair[c] = pair_start(c)
    for s in range(scans):
        first_half(1, s)
    place(1)
    grads_fold(1)
    copies_1 = grads_start(1, (4, 5, 6, 7, 2, 3))
    for c in early:
        row[c] = r_start(c, pair[c])
    for s in range(scans):
        second_half(1, s)
    for c in late:
        pair[c] = pair_start(c)
    place(0)
    grads_fold(0)
    copies_0 = grads_start(0, (4, 5, 6, 7, 2, 3))
    for c in late:
        row[c] = r_start(c, pair[c])
    copies_1 += grads_start(1, (0, 1))
    copies_0 += grads_start(0, (0, 1))
    for c in early:
        zed[c] = z_start(c, row[c])
    for c in late:
        zed[c] = z_start(c, row[c])
    for c in early:
        gat[c] = ag_start(c, zed[c])
    for c in late:
        gat[c] = ag_start(c, zed[c])
    grads_end(1, copies_1)
    grads_end(0, copies_0)
    for c in every:
        fw_start(c, *gat[c])
    for copy in sides_0 + ends_0 + sides_1 + ends_1 + copies_0 + copies_1:
        copy.wait_send()
    for c in every:
        for copy in [pair[c]] + row[c] + zed[c] + gat[c][0]:
            copy.wait_send()
    for c in every:
        for copy in gat[c][1]:
            copy.wait()
    full = total[...]
    scale = STEP_SIZE / jnp.sqrt(jnp.sum(full * full, keepdims=True) / full.size + EPSILON)
    for m in range(probe.shape[1]):
        for part in range(2):
            new_ref[part, m] = (
                probe[part, m] - scale * total[pl.ds((2 * m + part) * win, win)]
            )


def out_kernel(grad, new, grad_out, new_out, sem):
    copies = []
    for part in range(2):
        for lay in range(grad.shape[1]):
            copies.append((grad.at[part, lay], grad_out.at[part, lay]))
        copies.append((new.at[part], new_out.at[part]))
    copies = [
        pltpu.make_async_copy(src, dst, sem.at[i]) for i, (src, dst) in enumerate(copies)
    ]
    for copy in copies:
        copy.start()
    for copy in copies:
        copy.wait()


def on_device(object_tiles, probe_modes, offsets, amplitude):
    n_row, n_col = lax.axis_size("row"), lax.axis_size("col")
    n_z = n_col // 2
    tile, win, scans = object_tiles.shape[2], probe_modes.shape[2], offsets.shape[2]
    tall, nt = tile + 2 * HALO, tile // LANES
    modes = probe_modes.shape[1]
    g_rows = 2 * modes * win
    size = g_rows // CHUNKS
    chunks = tuple((i * size, size) for i in range(CHUNKS))
    piece = g_rows // 2 // n_row
    vmem = pl.BlockSpec(memory_space=pltpu.VMEM)
    hbm = pl.BlockSpec(memory_space=pltpu.HBM)
    dma = pltpu.SemaphoreType.DMA
    block = lambda *shape: pltpu.VMEM(shape, F32)
    pairs = offsets.transpose(0, 1, 3, 2)
    table = jnp.asarray(tables(win))
    grad, new = pl.pallas_call(
        functools.partial(fused_kernel, (n_row, n_col, win, scans, chunks)),
        out_shape=(
            jax.ShapeDtypeStruct(object_tiles.shape, F32),
            jax.ShapeDtypeStruct(probe_modes.shape, F32),
        ),
        in_specs=[hbm] * 5,
        out_specs=(vmem, vmem),
        scratch_shapes=[
            pltpu.SMEM(pairs.shape, jnp.int32),
            block(2, nt + 1, tall, LANES),
            block(2, nt + 1, tall, LANES),
            block(*probe_modes.shape),
            block(*amplitude.shape),
            pltpu.VMEM(table.shape, BF16),
            block(scans, 4, win, win),
            block(scans, 2, 2 * win, 2 * win),
            block(scans, 2, 2 * win, 2 * win),
            block(scans, win, win),
            block(2, 2, scans, win, win),
            block(g_rows, win),
            block(scans, 2, nt + 1, 2 * tall - win, LANES),
            block(2, 2, nt + 1, tall, LANES),
            block(2, tile // 2, LANES),
            block(2, tile // 2, LANES),
            block(2, tall // 2, LANES),
            block(2, tall // 2, LANES),
            block(2, 2, nt, HALO, LANES),
            block(2, 2, nt, HALO, LANES),
            block(2, tall // 2, LANES),
            block(2, tall // 2, LANES),
            block(2, tall // 2, LANES),
            block(2, tall // 2, LANES),
            block(g_rows // 2, win),
            block(g_rows // 2, win),
            block(n_row - 1, piece, win),
            block(n_z, piece, win),
            block(g_rows, win),
            dma((4 * nt + 4,)),
            dma((2, 8)),
            dma((2, 8)),
            dma((2, 8)),
            dma((2, 8)),
            dma((CHUNKS,)),
            dma((CHUNKS,)),
            dma((CHUNKS, n_row - 1)),
            dma((CHUNKS, n_row - 1)),
            dma((CHUNKS, n_z - 1)),
            dma((CHUNKS, n_z - 1)),
            dma((CHUNKS, n_row - 1)),
            dma((CHUNKS, n_row - 1)),
            dma((CHUNKS, n_row)),
            dma((CHUNKS, n_row)),
        ],
        compiler_params=pltpu.CompilerParams(
            collective_id=0, has_side_effects=True, vmem_limit_bytes=48 * 1024 * 1024
        ),
    )(
        *[
            pltpu.with_memory_space_constraint(x, pltpu.HBM)
            for x in (pairs, object_tiles, probe_modes, amplitude, table)
        ],
    )
    return pl.pallas_call(
        out_kernel,
        out_shape=(
            jax.ShapeDtypeStruct(object_tiles.shape, F32),
            jax.ShapeDtypeStruct(probe_modes.shape, F32),
        ),
        in_specs=[vmem, vmem],
        out_specs=(hbm, hbm),
        scratch_shapes=[dma((6,))],
        compiler_params=pltpu.CompilerParams(vmem_limit_bytes=1024 * 1024),
    )(grad, new)


CHUNKS = 2


def solution(mesh):
    placed = (
        P(None, None, "row", "col"),
        P(),
        P("row", "col", None, None),
        P("row", "col", None, None, None),
    )
    return jax.shard_map(
        on_device,
        mesh=mesh,
        in_specs=placed,
        out_specs=(P(None, None, "row", "col"), P()),
        check_vma=False,
    )
```

```python
import functools

import jax
import jax.numpy as jnp
import numpy as np
from jax import lax
from jax.experimental import pallas as pl
from jax.experimental.pallas import tpu as pltpu
from jax.sharding import PartitionSpec as P

HALO = 32
PROP = 0.002
SHIFT_AMP = 0.5
STEP_SIZE = 0.5
EPSILON = 1e-06
LANES = 128
SUB = 8
MESH = pl.DeviceIdType.MESH
F32 = jnp.float32
BF16 = jnp.bfloat16


def tables(win):
    k = np.arange(win)
    c = np.exp(-2j * np.pi * (k[:, None] * k[None, :] % win) / win) / np.sqrt(win)
    freq = (k + win // 2) % win - win // 2
    kern = np.conj(c) @ np.diag(np.exp(-1j * PROP * freq**2)) @ c
    out = []
    for m in (c, np.conj(c), kern, np.conj(kern)):
        full = np.block([[m.real, m.imag], [-m.imag, m.real]])
        high = full.astype(np.float32).astype(jnp.bfloat16)
        low = (full - high.astype(np.float64)).astype(np.float32).astype(jnp.bfloat16)
        out += [high, low]
    return np.stack(out)


FWD, INV, KER, KER_INV = 0, 1, 2, 3


def split(x):
    high = x.astype(BF16)
    return high, (x - high.astype(F32)).astype(BF16)


def dot(a, b):
    return jnp.dot(a, b, preferred_element_type=F32)


def right(x, tab, which):
    high, low = split(x)
    return dot(high, tab[2 * which]) + (
        dot(low, tab[2 * which]) + dot(high, tab[2 * which + 1])
    )


def left(x, tab, which):
    high, low = split(x)
    which = which ^ 1
    return dot(tab[2 * which], high) + (
        dot(tab[2 * which], low) + dot(tab[2 * which + 1], high)
    )


def swap(y):
    w = y.shape[0] // 2
    top = jnp.concatenate([y[:w, :w], y[w:, :w]], axis=1)
    low = jnp.concatenate([y[:w, w:], y[w:, w:]], axis=1)
    return jnp.concatenate([top, low], axis=0)


def twice(x, axis):
    return jnp.concatenate([x, x], axis=axis)


def lane(rows):
    return lax.broadcasted_iota(jnp.int32, (rows, LANES), 1)


FOLD = HALO // 2


def fold(get, rows, first):
    at = lane(rows // 2)
    out = None
    for part in range(2):
        x = get(part)
        for h in range(2):
            low = HALO * (2 * h + part)
            block = jnp.concatenate(
                [x[HALO * b + FOLD * h : HALO * b + FOLD * (h + 1)] for b in range(rows // HALO)],
                axis=0,
            )
            shift = (low - first) % LANES
            block = pltpu.roll(block, shift, 1) if shift else block
            keep = (at >= low) & (at < low + HALO)
            out = jnp.where(keep, block, 0.0 if out is None else out)
    return out


def unfold(x, part, first):
    halves = []
    for h in range(2):
        shift = (first - HALO * (2 * h + part)) % LANES
        halves.append(pltpu.roll(x, shift, 1) if shift else x)
    return jnp.concatenate(
        [
            halves[h][FOLD * b : FOLD * (b + 1)]
            for b in range(x.shape[0] // FOLD)
            for h in range(2)
        ],
        axis=0,
    )


def remote(src, dst, ssem, rsem, to):
    copy = pltpu.make_async_remote_copy(
        src_ref=src,
        dst_ref=dst,
        send_sem=ssem,
        recv_sem=rsem,
        device_id=to,
        device_id_type=MESH,
    )
    copy.start()
    return copy


def fused_kernel(
    sizes,
    off_hbm,
    obj_hbm,
    probe_hbm,
    amp_hbm,
    tab_hbm,
    grad_ref,
    total,
    probe,
    off_ref,
    ext_0,
    ext_1,
    amp,
    tab,
    winds,
    wave,
    far,
    factor,
    gobj,
    gprobe,
    zpad,
    acc,
    pack_l,
    pack_r,
    halo_l,
    halo_r,
    from_top,
    from_bot,
    edge_l,
    edge_r,
    from_l,
    from_r,
    half_in,
    half_sum,
    r_parts,
    z_parts,
    in_sem,
    h_send,
    h_recv,
    g_send,
    g_recv,
    pair_send,
    pair_recv,
    r_send,
    r_recv,
    z_send,
    z_recv,
    ag_send,
    ag_recv,
    fw_send,
    fw_recv,
):
    n_row, n_col, win, scans, chunks = sizes
    n_z = n_col // 2
    ext = (ext_0, ext_1)
    tile = grad_ref.shape[2]
    tall = tile + 2 * HALO
    nt = tile // LANES
    pad = tall - win
    my_r, my_c = lax.axis_index("row"), lax.axis_index("col")

    def at(dr, dc):
        return lax.rem(my_r + dr % n_row, n_row), lax.rem(my_c + dc % n_col, n_col)

    barrier = pltpu.get_barrier_semaphore()
    mates = {(dr % n_row, dc % n_col) for dr in (-1, 0, 1) for dc in (-1, 0, 1)}
    mates |= {(k, 0) for k in range(n_row)} | {(0, 2 * k) for k in range(n_z)}
    mates.discard((0, 0))
    for mate in sorted(mates):
        pl.semaphore_signal(barrier, inc=1, device_id=at(*mate), device_id_type=MESH)
    loads = []
    for lay in range(2):
        for part in range(2):
            for t in range(nt):
                loads.append(
                    pltpu.make_async_copy(
                        obj_hbm.at[part, lay, :, pl.ds(t * LANES, LANES)],
                        ext[lay].at[part, t, pl.ds(HALO, tile), :],
                        in_sem.at[len(loads)],
                    )
                )
    per_lay = len(loads) // 2
    for src, dst in ((off_hbm, off_ref), (probe_hbm, probe), (tab_hbm, tab), (amp_hbm, amp)):
        loads.append(pltpu.make_async_copy(src, dst, in_sem.at[len(loads)]))
    for load in loads:
        load.start()

    head, tail = pl.ds(0, FOLD), pl.ds((tile - HALO) // 2, FOLD)
    mid, after = pl.ds(FOLD, tile // 2), pl.ds(FOLD + tile // 2, FOLD)

    def pack(lay):
        for load in loads[lay * per_lay : (lay + 1) * per_lay]:
            load.wait()
        own = pl.ds(HALO, tile)
        pack_l[lay] = fold(lambda part: ext[lay][part, 0, own, :], tile, 0)
        pack_r[lay] = fold(lambda part: ext[lay][part, nt - 1, own, :], tile, LANES - HALO)

    def halo_start(lay, which):
        e, left_in, right_in = ext[lay], halo_l.at[lay], halo_r.at[lay]
        pl_, pr_ = pack_l.at[lay], pack_r.at[lay]
        own = pl.ds(0, nt)
        plan = [
            (e.at[:, own, pl.ds(tile, HALO)], e.at[:, own, pl.ds(0, HALO)], (1, 0)),
            (e.at[:, own, pl.ds(HALO, HALO)], e.at[:, own, pl.ds(HALO + tile, HALO)], (-1, 0)),
            (pr_, left_in.at[mid], (0, 1)),
            (pl_, right_in.at[mid], (0, -1)),
            (pr_.at[tail], left_in.at[head], (1, 1)),
            (pr_.at[head], left_in.at[after], (-1, 1)),
            (pl_.at[tail], right_in.at[head], (1, -1)),
            (pl_.at[head], right_in.at[after], (-1, -1)),
        ]
        return [
            remote(src, dst, h_send.at[lay, i], h_recv.at[lay, i], at(*to))
            for i, (src, dst, to) in ((i, plan[i]) for i in which)
        ]

    def halo_end(lay, copies, rows):
        for copy in copies:
            copy.wait_recv()
        for part in range(2):
            near = unfold(halo_r[lay], part, 0)
            distant = unfold(halo_l[lay], part, LANES - HALO)
            x = lane(tall)
            ext[lay][part, nt, pl.ds(0, tall), :] = jnp.where(
                x < HALO, near, jnp.where(x >= LANES - HALO, distant, 0.0)
            )
        for copy in rows:
            copy.wait_recv()

    def spot(s):
        row = off_ref[0, 0, 0, s]
        col = off_ref[0, 0, 1, s] - HALO
        col = jnp.where(col < 0, col + (nt + 1) * LANES, col)
        first = lax.div(col, LANES)
        second = jnp.where(first == nt, 0, first + 1)
        return row, first, second, col - first * LANES

    def windows(lay):
        for s in range(scans):
            row, first, second, rem = spot(s)
            for part in range(2):
                a = ext[lay][part, first, pl.ds(row, win), :]
                b = ext[lay][part, second, pl.ds(row, win), :]
                block = jnp.where(lane(win) >= rem, a, b)
                winds[s, 2 * part + lay] = pltpu.roll(block, lax.rem(LANES - rem, LANES), 1)

    sides, ends = (4, 5, 6, 7, 2, 3), (0, 1)
    pack(0)
    pack(1)
    pl.semaphore_wait(barrier, len(mates))
    sides_0 = halo_start(0, sides)
    sides_1 = halo_start(1, sides)
    ends_0 = halo_start(0, ends)
    ends_1 = halo_start(1, ends)
    gprobe[...] = jnp.zeros_like(gprobe)
    gobj[...] = jnp.zeros_like(gobj)
    zpad[...] = jnp.zeros_like(zpad)
    for load in loads[2 * per_lay :]:
        load.wait()
    halo_end(0, sides_0, ends_0)
    windows(0)

    for s in range(scans):
        or_, oi_ = winds[s, 0], winds[s, 2]
        for p in range(2):
            rows = []
            for m in range(2):
                pr, pi = probe[0, 2 * p + m], probe[1, 2 * p + m]
                rows.append(
                    jnp.concatenate([pr * or_ - pi * oi_, pr * oi_ + pi * or_], axis=1)
                )
            psi = jnp.concatenate(rows, axis=0)
            wave[s, p] = left(swap(right(psi, tab, KER)), tab, KER)

    halo_end(1, sides_1, ends_1)
    windows(1)

    for s in range(scans):
        power = None
        for p in range(2):
            w = wave[s, p]
            wr, wi = w[:win], w[win:]
            o1r, o1i = twice(winds[s, 1], 1), twice(winds[s, 3], 1)
            psi = jnp.concatenate([wr * o1r - wi * o1i, wr * o1i + wi * o1r], axis=0)
            psi = right(swap(left(psi, tab, FWD)), tab, FWD)
            far[s, p] = psi
            sq = psi * psi
            part_sum = (sq[:win, :win] + sq[:win, win:]) + (sq[win:, :win] + sq[win:, win:])
            power = part_sum if power is None else power + part_sum
        root = jnp.sqrt(power + SHIFT_AMP)
        factor[s] = 2.0 * (root - amp[0, 0, s]) / root

    def first_half(p, s):
        g = far[s, p] * twice(twice(factor[s], 0), 1)
        g = left(swap(right(g, tab, INV)), tab, INV)
        w = wave[s, p]
        gr, gi, wr, wi = g[:win], g[win:], w[:win], w[win:]
        re = wr * gr + wi * gi
        im = wr * gi - wi * gr
        gobj[1, 0, s] += re[:, :win] + re[:, win:]
        gobj[1, 1, s] += im[:, :win] + im[:, win:]
        o1r, o1i = twice(winds[s, 1], 1), twice(winds[s, 3], 1)
        far[s, p] = jnp.concatenate([o1r * gr + o1i * gi, o1r * gi - o1i * gr], axis=0)

    def second_half(p, s):
        g = right(swap(left(far[s, p], tab, KER_INV)), tab, KER_INV)
        o0r, o0i = winds[s, 0], winds[s, 2]
        re = im = None
        for m in range(2):
            gr, gi = g[m * win : (m + 1) * win, :win], g[m * win : (m + 1) * win, win:]
            pr, pi = probe[0, 2 * p + m], probe[1, 2 * p + m]
            a = pr * gr + pi * gi
            b = pr * gi - pi * gr
            re, im = (a, b) if re is None else (re + a, im + b)
            base = (2 * p + m) * 2 * win
            gprobe[pl.ds(base, win)] += o0r * gr + o0i * gi
            gprobe[pl.ds(base + win, win)] += o0r * gi - o0i * gr
        gobj[0, 0, s] += re
        gobj[0, 1, s] += im

    def place(lay):
        starts = []
        for s in range(scans):
            row, first, second, rem = spot(s)
            starts.append(pad - row)
            where = jnp.where(lane(win) >= rem, first, second)
            for part in range(2):
                block = pltpu.roll(gobj[lay, part, s], rem, 1)
                for t in range(nt + 1):
                    zpad[s, part, t, pl.ds(pad, win), :] = jnp.where(where == t, block, 0.0)
        for part in range(2):
            for t in range(nt + 1):
                value = None
                for s in range(scans):
                    block = zpad[s, part, t, pl.ds(starts[s], tall), :]
                    value = block if value is None else value + block
                acc[lay, part, t] = value

    def grads_fold(lay):
        edge_r[lay] = fold(lambda part: acc[lay, part, nt], tall, 0)
        edge_l[lay] = fold(lambda part: acc[lay, part, nt], tall, LANES - HALO)

    def grads_start(lay, which):
        a, er, el = acc.at[lay], edge_r.at[lay], edge_l.at[lay]
        fl, fr = from_l.at[lay], from_r.at[lay]
        own = pl.ds(0, nt)
        plan = [
            (a.at[:, own, pl.ds(0, HALO)], from_bot.at[lay], (-1, 0)),
            (a.at[:, own, pl.ds(HALO + tile, HALO)], from_top.at[lay], (1, 0)),
            (er.at[mid], fl.at[mid], (0, 1)),
            (el.at[mid], fr.at[mid], (0, -1)),
            (er.at[head], fl.at[after], (-1, 1)),
            (er.at[after], fl.at[head], (1, 1)),
            (el.at[head], fr.at[after], (-1, -1)),
            (el.at[after], fr.at[head], (1, -1)),
        ]
        return [
            remote(src, dst, g_send.at[lay, i], g_recv.at[lay, i], at(*to))
            for i, (src, dst, to) in ((i, plan[i]) for i in which)
        ]

    def grads_end(lay, copies):
        for copy in copies:
            copy.wait_recv()
        x = lane(tall)
        for part in range(2):
            for t in range(nt):
                value = acc[lay, part, t, pl.ds(HALO, tile), :]
                top, bot = from_top[lay, part, t], from_bot[lay, part, t]
                for ref, first, edge in ((from_l, 0, 0), (from_r, LANES - HALO, nt - 1)):
                    if t == edge:
                        block = unfold(ref[lay], part, first)
                        block = jnp.where((x >= first) & (x < first + HALO), block, 0.0)
                        value = value + block[HALO : HALO + tile]
                        top = top + block[:HALO]
                        bot = bot + block[HALO + tile :]
                cols = pl.ds(t * LANES, LANES)
                grad_ref[part, lay, pl.ds(0, HALO), cols] = value[:HALO] + top
                grad_ref[part, lay, pl.ds(HALO, tile - 2 * HALO), cols] = value[HALO:-HALO]
                grad_ref[part, lay, pl.ds(tile - HALO, HALO), cols] = value[-HALO:] + bot

    odd = lax.rem(my_c, 2)
    partner = (my_r, my_c + 1 - 2 * odd)
    my_z = lax.div(my_c, 2)

    def span(c):
        start, size = chunks[c]
        half = size // 2
        piece = half // n_row
        return start, half, piece, start // 2, start // 2 // n_row

    def rows_at(start, size):
        return pl.ds(pl.multiple_of(start, SUB), size)

    def row_mate(k):
        return lax.rem(my_r + k, n_row)

    def pair_start(c):
        start, half, piece, hs, ps = span(c)
        return remote(
            gprobe.at[rows_at(start + (1 - odd) * half, half)],
            half_in.at[pl.ds(hs, half)],
            pair_send.at[c],
            pair_recv.at[c],
            partner,
        )

    def r_start(c, pair):
        start, half, piece, hs, ps = span(c)
        pair.wait_recv()
        half_sum[pl.ds(hs, half)] = (
            gprobe[rows_at(start + odd * half, half)] + half_in[pl.ds(hs, half)]
        )
        copies = []
        for k in range(1, n_row):
            q = row_mate(k)
            copies.append(
                remote(
                    half_sum.at[rows_at(hs + q * piece, piece)],
                    r_parts.at[k - 1, pl.ds(ps, piece)],
                    r_send.at[c, k - 1],
                    r_recv.at[c, k - 1],
                    (q, my_c),
                )
            )
        return copies

    def z_start(c, before):
        start, half, piece, hs, ps = span(c)
        for copy in before:
            copy.wait_recv()
        value = half_sum[rows_at(hs + my_r * piece, piece)]
        for k in range(n_row - 1):
            value = value + r_parts[k, pl.ds(ps, piece)]
        z_parts[my_z, pl.ds(ps, piece)] = value
        mine = z_parts.at[my_z, pl.ds(ps, piece)]
        return [
            remote(mine, mine, z_send.at[c, k - 1], z_recv.at[c, k - 1], at(0, 2 * k))
            for k in range(1, n_z)
        ]

    def ag_start(c, before):
        start, half, piece, hs, ps = span(c)
        for copy in before:
            copy.wait_recv()
        value = z_parts[0, pl.ds(ps, piece)]
        for k in range(1, n_z):
            value = value + z_parts[k, pl.ds(ps, piece)]
        own = rows_at(start + odd * half + my_r * piece, piece)
        total[own] = value
        mine = total.at[own]
        copies = [
            remote(mine, mine, ag_send.at[c, k - 1], ag_recv.at[c, k - 1], at(k, 0))
            for k in range(1, n_row)
        ]
        return copies, [remote(mine, mine, fw_send.at[c, 0], fw_recv.at[c, 0], partner)]

    def fw_start(c, copies, forwards):
        start, half, piece, hs, ps = span(c)
        for k in range(1, n_row):
            copies[k - 1].wait_recv()
            q = lax.rem(my_r + n_row - k, n_row)
            got = total.at[rows_at(start + odd * half + q * piece, piece)]
            forwards.append(remote(got, got, fw_send.at[c, k], fw_recv.at[c, k], partner))

    early, late = range(len(chunks) // 2), range(len(chunks) // 2, len(chunks))
    every = range(len(chunks))
    pair, row, zed, gat = {}, {}, {}, {}
    for s in range(scans):
        first_half(0, s)
    for s in range(scans):
        second_half(0, s)
    for c in early:
        pair[c] = pair_start(c)
    for s in range(scans):
        first_half(1, s)
    place(1)
    grads_fold(1)
    copies_1 = grads_start(1, (4, 5, 6, 7, 2, 3))
    for c in early:
        row[c] = r_start(c, pair[c])
    for s in range(scans):
        second_half(1, s)
    for c in late:
        pair[c] = pair_start(c)
    place(0)
    grads_fold(0)
    copies_0 = grads_start(0, (4, 5, 6, 7, 2, 3))
    for c in late:
        row[c] = r_start(c, pair[c])
    copies_1 += grads_start(1, (0, 1))
    copies_0 += grads_start(0, (0, 1))
    for c in early:
        zed[c] = z_start(c, row[c])
    for c in late:
        zed[c] = z_start(c, row[c])
    for c in early:
        gat[c] = ag_start(c, zed[c])
    for c in late:
        gat[c] = ag_start(c, zed[c])
    grads_end(1, copies_1)
    grads_end(0, copies_0)
    for c in every:
        fw_start(c, *gat[c])
    for copy in sides_0 + ends_0 + sides_1 + ends_1 + copies_0 + copies_1:
        copy.wait_send()
    for c in every:
        for copy in [pair[c]] + row[c] + zed[c] + gat[c][0]:
            copy.wait_send()
    for c in every:
        for copy in gat[c][1]:
            copy.wait()


def out_kernel(grad, total, probe, grad_out, new_out, new, sem):
    count = grad.shape[1]
    copies = [
        pltpu.make_async_copy(grad.at[i, j], grad_out.at[i, j], sem.at[i * count + j])
        for i in range(2)
        for j in range(count)
    ]
    for copy in copies:
        copy.start()
    full = total[...]
    win = probe.shape[2]
    scale = STEP_SIZE / jnp.sqrt(jnp.sum(full * full, keepdims=True) / full.size + EPSILON)
    for part in range(2):
        for m in range(probe.shape[1]):
            new[part, m] = probe[part, m] - scale * total[pl.ds((2 * m + part) * win, win)]
        copy = pltpu.make_async_copy(new.at[part], new_out.at[part], sem.at[2 * count + part])
        copy.start()
        copies.append(copy)
    for copy in copies:
        copy.wait()


def on_device(object_tiles, probe_modes, offsets, amplitude):
    n_row, n_col = lax.axis_size("row"), lax.axis_size("col")
    n_z = n_col // 2
    tile, win, scans = object_tiles.shape[2], probe_modes.shape[2], offsets.shape[2]
    tall, nt = tile + 2 * HALO, tile // LANES
    modes = probe_modes.shape[1]
    g_rows = 2 * modes * win
    size = g_rows // CHUNKS
    chunks = tuple((i * size, size) for i in range(CHUNKS))
    piece = g_rows // 2 // n_row
    vmem = pl.BlockSpec(memory_space=pltpu.VMEM)
    hbm = pl.BlockSpec(memory_space=pltpu.HBM)
    dma = pltpu.SemaphoreType.DMA
    block = lambda *shape: pltpu.VMEM(shape, F32)
    pairs = offsets.transpose(0, 1, 3, 2)
    table = jnp.asarray(tables(win))
    grad, total, probe = pl.pallas_call(
        functools.partial(fused_kernel, (n_row, n_col, win, scans, chunks)),
        out_shape=(
            jax.ShapeDtypeStruct(object_tiles.shape, F32),
            jax.ShapeDtypeStruct((g_rows, win), F32),
            jax.ShapeDtypeStruct(probe_modes.shape, F32),
        ),
        in_specs=[hbm] * 5,
        out_specs=(vmem, vmem, vmem),
        scratch_shapes=[
            pltpu.SMEM(pairs.shape, jnp.int32),
            block(2, nt + 1, tall, LANES),
            block(2, nt + 1, tall, LANES),
            block(*amplitude.shape),
            pltpu.VMEM(table.shape, BF16),
            block(scans, 4, win, win),
            block(scans, 2, 2 * win, 2 * win),
            block(scans, 2, 2 * win, 2 * win),
            block(scans, win, win),
            block(2, 2, scans, win, win),
            block(g_rows, win),
            block(scans, 2, nt + 1, 2 * tall - win, LANES),
            block(2, 2, nt + 1, tall, LANES),
            block(2, tile // 2, LANES),
            block(2, tile // 2, LANES),
            block(2, tall // 2, LANES),
            block(2, tall // 2, LANES),
            block(2, 2, nt, HALO, LANES),
            block(2, 2, nt, HALO, LANES),
            block(2, tall // 2, LANES),
            block(2, tall // 2, LANES),
            block(2, tall // 2, LANES),
            block(2, tall // 2, LANES),
            block(g_rows // 2, win),
            block(g_rows // 2, win),
            block(n_row - 1, piece, win),
            block(n_z, piece, win),
            dma((4 * nt + 4,)),
            dma((2, 8)),
            dma((2, 8)),
            dma((2, 8)),
            dma((2, 8)),
            dma((CHUNKS,)),
            dma((CHUNKS,)),
            dma((CHUNKS, n_row - 1)),
            dma((CHUNKS, n_row - 1)),
            dma((CHUNKS, n_z - 1)),
            dma((CHUNKS, n_z - 1)),
            dma((CHUNKS, n_row - 1)),
            dma((CHUNKS, n_row - 1)),
            dma((CHUNKS, n_row)),
            dma((CHUNKS, n_row)),
        ],
        compiler_params=pltpu.CompilerParams(
            collective_id=0, has_side_effects=True, vmem_limit_bytes=48 * 1024 * 1024
        ),
    )(
        *[
            pltpu.with_memory_space_constraint(x, pltpu.HBM)
            for x in (pairs, object_tiles, probe_modes, amplitude, table)
        ],
    )
    return pl.pallas_call(
        out_kernel,
        out_shape=(
            jax.ShapeDtypeStruct(object_tiles.shape, F32),
            jax.ShapeDtypeStruct(probe_modes.shape, F32),
        ),
        in_specs=[vmem, vmem, vmem],
        out_specs=(hbm, hbm),
        scratch_shapes=[block(*probe_modes.shape), dma((2 * object_tiles.shape[1] + 2,))],
        compiler_params=pltpu.CompilerParams(vmem_limit_bytes=4 * 1024 * 1024),
    )(grad, total, probe)


CHUNKS = 2


def solution(mesh):
    placed = (
        P(None, None, "row", "col"),
        P(),
        P("row", "col", None, None),
        P("row", "col", None, None, None),
    )
    return jax.shard_map(
        on_device,
        mesh=mesh,
        in_specs=placed,
        out_specs=(P(None, None, "row", "col"), P()),
        check_vma=False,
    )
```

```python
import functools

import jax
import jax.numpy as jnp
import numpy as np
from jax import lax
from jax.experimental import pallas as pl
from jax.experimental.pallas import tpu as pltpu
from jax.sharding import PartitionSpec as P

HALO = 32
PROP = 0.002
SHIFT_AMP = 0.5
STEP_SIZE = 0.5
EPSILON = 1e-06
LANES = 128
SUB = 8
MESH = pl.DeviceIdType.MESH
F32 = jnp.float32
BF16 = jnp.bfloat16


def tables(win):
    k = np.arange(win)
    c = np.exp(-2j * np.pi * (k[:, None] * k[None, :] % win) / win) / np.sqrt(win)
    freq = (k + win // 2) % win - win // 2
    kern = np.conj(c) @ np.diag(np.exp(-1j * PROP * freq**2)) @ c
    out = []
    for m in (c, np.conj(c), kern, np.conj(kern)):
        full = np.block([[m.real, m.imag], [-m.imag, m.real]])
        high = full.astype(np.float32).astype(jnp.bfloat16)
        low = (full - high.astype(np.float64)).astype(np.float32).astype(jnp.bfloat16)
        out += [high, low]
    return np.stack(out)


FWD, INV, KER, KER_INV = 0, 1, 2, 3


def split(x):
    high = x.astype(BF16)
    return high, (x - high.astype(F32)).astype(BF16)


def dot(a, b):
    return jnp.dot(a, b, preferred_element_type=F32)


def right(x, tab, which):
    high, low = split(x)
    return dot(high, tab[2 * which]) + (
        dot(low, tab[2 * which]) + dot(high, tab[2 * which + 1])
    )


def left(x, tab, which):
    high, low = split(x)
    which = which ^ 1
    return dot(tab[2 * which], high) + (
        dot(tab[2 * which], low) + dot(tab[2 * which + 1], high)
    )


def swap(y):
    w = y.shape[0] // 2
    top = jnp.concatenate([y[:w, :w], y[w:, :w]], axis=1)
    low = jnp.concatenate([y[:w, w:], y[w:, w:]], axis=1)
    return jnp.concatenate([top, low], axis=0)


def twice(x, axis):
    return jnp.concatenate([x, x], axis=axis)


def lane(rows):
    return lax.broadcasted_iota(jnp.int32, (rows, LANES), 1)


FOLD = HALO // 2


def fold(get, rows, first):
    at = lane(rows // 2)
    out = None
    for part in range(2):
        x = get(part)
        for h in range(2):
            low = HALO * (2 * h + part)
            block = jnp.concatenate(
                [x[HALO * b + FOLD * h : HALO * b + FOLD * (h + 1)] for b in range(rows // HALO)],
                axis=0,
            )
            shift = (low - first) % LANES
            block = pltpu.roll(block, shift, 1) if shift else block
            keep = (at >= low) & (at < low + HALO)
            out = jnp.where(keep, block, 0.0 if out is None else out)
    return out


def unfold(x, part, first):
    halves = []
    for h in range(2):
        shift = (first - HALO * (2 * h + part)) % LANES
        halves.append(pltpu.roll(x, shift, 1) if shift else x)
    return jnp.concatenate(
        [
            halves[h][FOLD * b : FOLD * (b + 1)]
            for b in range(x.shape[0] // FOLD)
            for h in range(2)
        ],
        axis=0,
    )


def remote(src, dst, ssem, rsem, to):
    copy = pltpu.make_async_remote_copy(
        src_ref=src,
        dst_ref=dst,
        send_sem=ssem,
        recv_sem=rsem,
        device_id=to,
        device_id_type=MESH,
    )
    copy.start()
    return copy


def fused_kernel(
    sizes,
    off_hbm,
    obj_hbm,
    probe_hbm,
    amp_hbm,
    tab_hbm,
    grad_ref,
    total,
    probe,
    off_ref,
    ext_0,
    ext_1,
    amp,
    tab,
    winds,
    wave,
    far,
    factor,
    gobj,
    gprobe,
    zpad,
    acc,
    pack_l,
    pack_r,
    halo_l,
    halo_r,
    from_top,
    from_bot,
    edge_l,
    edge_r,
    from_l,
    from_r,
    half_in,
    half_sum,
    r_parts,
    z_parts,
    in_sem,
    h_send,
    h_recv,
    g_send,
    g_recv,
    pair_send,
    pair_recv,
    r_send,
    r_recv,
    z_send,
    z_recv,
    ag_send,
    ag_recv,
    fw_send,
    fw_recv,
):
    n_row, n_col, win, scans, chunks = sizes
    n_z = n_col // 2
    ext = (ext_0, ext_1)
    tile = grad_ref.shape[2]
    tall = tile + 2 * HALO
    nt = tile // LANES
    pad = tall - win
    my_r, my_c = lax.axis_index("row"), lax.axis_index("col")

    def at(dr, dc):
        return lax.rem(my_r + dr % n_row, n_row), lax.rem(my_c + dc % n_col, n_col)

    barrier = pltpu.get_barrier_semaphore()
    mates = {(dr % n_row, dc % n_col) for dr in (-1, 0, 1) for dc in (-1, 0, 1)}
    mates |= {(k, 0) for k in range(n_row)} | {(0, 2 * k) for k in range(n_z)}
    mates.discard((0, 0))
    hops = lambda mate: min(mate[0], n_row - mate[0]) + min(mate[1], n_col - mate[1])
    for mate in sorted(sorted(mates), key=hops, reverse=True):
        pl.semaphore_signal(barrier, inc=1, device_id=at(*mate), device_id_type=MESH)
    loads = []
    for lay in range(2):
        for part in range(2):
            for t in range(nt):
                loads.append(
                    pltpu.make_async_copy(
                        obj_hbm.at[part, lay, :, pl.ds(t * LANES, LANES)],
                        ext[lay].at[part, t, pl.ds(HALO, tile), :],
                        in_sem.at[len(loads)],
                    )
                )
    per_lay = len(loads) // 2
    for src, dst in ((off_hbm, off_ref), (probe_hbm, probe), (tab_hbm, tab), (amp_hbm, amp)):
        loads.append(pltpu.make_async_copy(src, dst, in_sem.at[len(loads)]))
    for load in loads[: 2 * per_lay + 1]:
        load.start()

    head, tail = pl.ds(0, FOLD), pl.ds((tile - HALO) // 2, FOLD)
    mid, after = pl.ds(FOLD, tile // 2), pl.ds(FOLD + tile // 2, FOLD)

    def pack(lay):
        for load in loads[lay * per_lay : (lay + 1) * per_lay]:
            load.wait()
        own = pl.ds(HALO, tile)
        pack_l[lay] = fold(lambda part: ext[lay][part, 0, own, :], tile, 0)
        pack_r[lay] = fold(lambda part: ext[lay][part, nt - 1, own, :], tile, LANES - HALO)

    def halo_start(lay, which):
        e, left_in, right_in = ext[lay], halo_l.at[lay], halo_r.at[lay]
        pl_, pr_ = pack_l.at[lay], pack_r.at[lay]
        own = pl.ds(0, nt)
        plan = [
            (e.at[:, own, pl.ds(tile, HALO)], e.at[:, own, pl.ds(0, HALO)], (1, 0)),
            (e.at[:, own, pl.ds(HALO, HALO)], e.at[:, own, pl.ds(HALO + tile, HALO)], (-1, 0)),
            (pr_, left_in.at[mid], (0, 1)),
            (pl_, right_in.at[mid], (0, -1)),
            (pr_.at[tail], left_in.at[head], (1, 1)),
            (pr_.at[head], left_in.at[after], (-1, 1)),
            (pl_.at[tail], right_in.at[head], (1, -1)),
            (pl_.at[head], right_in.at[after], (-1, -1)),
        ]
        return [
            remote(src, dst, h_send.at[lay, i], h_recv.at[lay, i], at(*to))
            for i, (src, dst, to) in ((i, plan[i]) for i in which)
        ]

    def halo_end(lay, copies, rows):
        for copy in copies:
            copy.wait_recv()
        for part in range(2):
            near = unfold(halo_r[lay], part, 0)
            distant = unfold(halo_l[lay], part, LANES - HALO)
            x = lane(tall)
            ext[lay][part, nt, pl.ds(0, tall), :] = jnp.where(
                x < HALO, near, jnp.where(x >= LANES - HALO, distant, 0.0)
            )
        for copy in rows:
            copy.wait_recv()

    def spot(s):
        row = off_ref[0, 0, 0, s]
        col = off_ref[0, 0, 1, s] - HALO
        col = jnp.where(col < 0, col + (nt + 1) * LANES, col)
        first = lax.div(col, LANES)
        second = jnp.where(first == nt, 0, first + 1)
        return row, first, second, col - first * LANES

    def windows(lay):
        for s in range(scans):
            row, first, second, rem = spot(s)
            for part in range(2):
                a = ext[lay][part, first, pl.ds(row, win), :]
                b = ext[lay][part, second, pl.ds(row, win), :]
                block = jnp.where(lane(win) >= rem, a, b)
                winds[s, 2 * part + lay] = pltpu.roll(block, lax.rem(LANES - rem, LANES), 1)

    sides, ends = (4, 5, 6, 7, 2, 3), (0, 1)
    pack(0)
    pack(1)
    pl.semaphore_wait(barrier, len(mates))
    sides_0 = halo_start(0, sides)
    sides_1 = halo_start(1, sides)
    ends_0 = halo_start(0, ends)
    ends_1 = halo_start(1, ends)
    for load in loads[2 * per_lay + 1 :]:
        load.start()
    gprobe[...] = jnp.zeros_like(gprobe)
    gobj[...] = jnp.zeros_like(gobj)
    zpad[...] = jnp.zeros_like(zpad)
    for load in loads[2 * per_lay :]:
        load.wait()
    halo_end(0, sides_0, ends_0)
    windows(0)

    for s in range(scans):
        or_, oi_ = winds[s, 0], winds[s, 2]
        for p in range(2):
            rows = []
            for m in range(2):
                pr, pi = probe[0, 2 * p + m], probe[1, 2 * p + m]
                rows.append(
                    jnp.concatenate([pr * or_ - pi * oi_, pr * oi_ + pi * or_], axis=1)
                )
            psi = jnp.concatenate(rows, axis=0)
            wave[s, p] = left(swap(right(psi, tab, KER)), tab, KER)

    halo_end(1, sides_1, ends_1)
    windows(1)

    for s in range(scans):
        power = None
        for p in range(2):
            w = wave[s, p]
            wr, wi = w[:win], w[win:]
            o1r, o1i = twice(winds[s, 1], 1), twice(winds[s, 3], 1)
            psi = jnp.concatenate([wr * o1r - wi * o1i, wr * o1i + wi * o1r], axis=0)
            psi = right(swap(left(psi, tab, FWD)), tab, FWD)
            far[s, p] = psi
            sq = psi * psi
            part_sum = (sq[:win, :win] + sq[:win, win:]) + (sq[win:, :win] + sq[win:, win:])
            power = part_sum if power is None else power + part_sum
        root = jnp.sqrt(power + SHIFT_AMP)
        factor[s] = 2.0 * (root - amp[0, 0, s]) / root

    def first_half(p, s):
        g = far[s, p] * twice(twice(factor[s], 0), 1)
        g = left(swap(right(g, tab, INV)), tab, INV)
        w = wave[s, p]
        gr, gi, wr, wi = g[:win], g[win:], w[:win], w[win:]
        re = wr * gr + wi * gi
        im = wr * gi - wi * gr
        gobj[1, 0, s] += re[:, :win] + re[:, win:]
        gobj[1, 1, s] += im[:, :win] + im[:, win:]
        o1r, o1i = twice(winds[s, 1], 1), twice(winds[s, 3], 1)
        far[s, p] = jnp.concatenate([o1r * gr + o1i * gi, o1r * gi - o1i * gr], axis=0)

    def second_half(p, s):
        g = right(swap(left(far[s, p], tab, KER_INV)), tab, KER_INV)
        o0r, o0i = winds[s, 0], winds[s, 2]
        re = im = None
        for m in range(2):
            gr, gi = g[m * win : (m + 1) * win, :win], g[m * win : (m + 1) * win, win:]
            pr, pi = probe[0, 2 * p + m], probe[1, 2 * p + m]
            a = pr * gr + pi * gi
            b = pr * gi - pi * gr
            re, im = (a, b) if re is None else (re + a, im + b)
            base = (2 * p + m) * 2 * win
            gprobe[pl.ds(base, win)] += o0r * gr + o0i * gi
            gprobe[pl.ds(base + win, win)] += o0r * gi - o0i * gr
        gobj[0, 0, s] += re
        gobj[0, 1, s] += im

    def place(lay):
        starts = []
        for s in range(scans):
            row, first, second, rem = spot(s)
            starts.append(pad - row)
            where = jnp.where(lane(win) >= rem, first, second)
            for part in range(2):
                block = pltpu.roll(gobj[lay, part, s], rem, 1)
                for t in range(nt + 1):
                    zpad[s, part, t, pl.ds(pad, win), :] = jnp.where(where == t, block, 0.0)
        for part in range(2):
            for t in range(nt + 1):
                value = None
                for s in range(scans):
                    block = zpad[s, part, t, pl.ds(starts[s], tall), :]
                    value = block if value is None else value + block
                acc[lay, part, t] = value

    def grads_fold(lay):
        edge_r[lay] = fold(lambda part: acc[lay, part, nt], tall, 0)
        edge_l[lay] = fold(lambda part: acc[lay, part, nt], tall, LANES - HALO)

    def grads_start(lay, which):
        a, er, el = acc.at[lay], edge_r.at[lay], edge_l.at[lay]
        fl, fr = from_l.at[lay], from_r.at[lay]
        own = pl.ds(0, nt)
        plan = [
            (a.at[:, own, pl.ds(0, HALO)], from_bot.at[lay], (-1, 0)),
            (a.at[:, own, pl.ds(HALO + tile, HALO)], from_top.at[lay], (1, 0)),
            (er.at[mid], fl.at[mid], (0, 1)),
            (el.at[mid], fr.at[mid], (0, -1)),
            (er.at[head], fl.at[after], (-1, 1)),
            (er.at[after], fl.at[head], (1, 1)),
            (el.at[head], fr.at[after], (-1, -1)),
            (el.at[after], fr.at[head], (1, -1)),
        ]
        return [
            remote(src, dst, g_send.at[lay, i], g_recv.at[lay, i], at(*to))
            for i, (src, dst, to) in ((i, plan[i]) for i in which)
        ]

    def grads_end(lay, copies):
        for copy in copies:
            copy.wait_recv()
        x = lane(tall)
        for part in range(2):
            for t in range(nt):
                value = acc[lay, part, t, pl.ds(HALO, tile), :]
                top, bot = from_top[lay, part, t], from_bot[lay, part, t]
                for ref, first, edge in ((from_l, 0, 0), (from_r, LANES - HALO, nt - 1)):
                    if t == edge:
                        block = unfold(ref[lay], part, first)
                        block = jnp.where((x >= first) & (x < first + HALO), block, 0.0)
                        value = value + block[HALO : HALO + tile]
                        top = top + block[:HALO]
                        bot = bot + block[HALO + tile :]
                cols = pl.ds(t * LANES, LANES)
                grad_ref[part, lay, pl.ds(0, HALO), cols] = value[:HALO] + top
                grad_ref[part, lay, pl.ds(HALO, tile - 2 * HALO), cols] = value[HALO:-HALO]
                grad_ref[part, lay, pl.ds(tile - HALO, HALO), cols] = value[-HALO:] + bot

    odd = lax.rem(my_c, 2)
    partner = (my_r, my_c + 1 - 2 * odd)
    my_z = lax.div(my_c, 2)

    def span(c):
        start, size = chunks[c]
        half = size // 2
        piece = half // n_row
        return start, half, piece, start // 2, start // 2 // n_row

    def rows_at(start, size):
        return pl.ds(pl.multiple_of(start, SUB), size)

    def row_mate(k):
        return lax.rem(my_r + k, n_row)

    def pair_start(c):
        start, half, piece, hs, ps = span(c)
        return remote(
            gprobe.at[rows_at(start + (1 - odd) * half, half)],
            half_in.at[pl.ds(hs, half)],
            pair_send.at[c],
            pair_recv.at[c],
            partner,
        )

    def r_start(c, pair):
        start, half, piece, hs, ps = span(c)
        pair.wait_recv()
        half_sum[pl.ds(hs, half)] = (
            gprobe[rows_at(start + odd * half, half)] + half_in[pl.ds(hs, half)]
        )
        copies = []
        for k in range(1, n_row):
            q = row_mate(k)
            copies.append(
                remote(
                    half_sum.at[rows_at(hs + q * piece, piece)],
                    r_parts.at[k - 1, pl.ds(ps, piece)],
                    r_send.at[c, k - 1],
                    r_recv.at[c, k - 1],
                    (q, my_c),
                )
            )
        return copies

    def z_start(c, before):
        start, half, piece, hs, ps = span(c)
        for copy in before:
            copy.wait_recv()
        value = half_sum[rows_at(hs + my_r * piece, piece)]
        for k in range(n_row - 1):
            value = value + r_parts[k, pl.ds(ps, piece)]
        z_parts[my_z, pl.ds(ps, piece)] = value
        mine = z_parts.at[my_z, pl.ds(ps, piece)]
        return [
            remote(mine, mine, z_send.at[c, k - 1], z_recv.at[c, k - 1], at(0, 2 * k))
            for k in range(1, n_z)
        ]

    def ag_start(c, before):
        start, half, piece, hs, ps = span(c)
        for copy in before:
            copy.wait_recv()
        value = z_parts[0, pl.ds(ps, piece)]
        for k in range(1, n_z):
            value = value + z_parts[k, pl.ds(ps, piece)]
        own = rows_at(start + odd * half + my_r * piece, piece)
        total[own] = value
        mine = total.at[own]
        copies = [
            remote(mine, mine, ag_send.at[c, k - 1], ag_recv.at[c, k - 1], at(k, 0))
            for k in range(1, n_row)
        ]
        return copies, [remote(mine, mine, fw_send.at[c, 0], fw_recv.at[c, 0], partner)]

    def fw_start(c, copies, forwards):
        start, half, piece, hs, ps = span(c)
        for k in range(1, n_row):
            copies[k - 1].wait_recv()
            q = lax.rem(my_r + n_row - k, n_row)
            got = total.at[rows_at(start + odd * half + q * piece, piece)]
            forwards.append(remote(got, got, fw_send.at[c, k], fw_recv.at[c, k], partner))

    early, late = range(len(chunks) // 2), range(len(chunks) // 2, len(chunks))
    every = range(len(chunks))
    pair, row, zed, gat = {}, {}, {}, {}
    for s in range(scans):
        first_half(0, s)
    for s in range(scans):
        second_half(0, s)
    for c in early:
        pair[c] = pair_start(c)
    for s in range(scans):
        first_half(1, s)
    place(1)
    grads_fold(1)
    copies_1 = grads_start(1, (4, 5, 6, 7, 2, 3))
    for c in early:
        row[c] = r_start(c, pair[c])
    for s in range(scans):
        second_half(1, s)
    for c in late:
        pair[c] = pair_start(c)
    place(0)
    grads_fold(0)
    copies_0 = grads_start(0, (4, 5, 6, 7, 2, 3))
    for c in late:
        row[c] = r_start(c, pair[c])
    copies_1 += grads_start(1, (0, 1))
    copies_0 += grads_start(0, (0, 1))
    for c in early:
        zed[c] = z_start(c, row[c])
    for c in late:
        zed[c] = z_start(c, row[c])
    for c in early:
        gat[c] = ag_start(c, zed[c])
    for c in late:
        gat[c] = ag_start(c, zed[c])
    grads_end(1, copies_1)
    grads_end(0, copies_0)
    for c in every:
        fw_start(c, *gat[c])
    for copy in sides_0 + ends_0 + sides_1 + ends_1 + copies_0 + copies_1:
        copy.wait_send()
    for c in every:
        for copy in [pair[c]] + row[c] + zed[c] + gat[c][0]:
            copy.wait_send()
    for c in every:
        for copy in gat[c][1]:
            copy.wait()


def out_kernel(grad, total, probe, grad_out, new_out, new, sem):
    count = grad.shape[1]
    copies = [
        pltpu.make_async_copy(grad.at[i, j], grad_out.at[i, j], sem.at[i * count + j])
        for i in range(2)
        for j in range(count)
    ]
    for copy in copies:
        copy.start()
    full = total[...]
    win = probe.shape[2]
    scale = STEP_SIZE / jnp.sqrt(jnp.sum(full * full, keepdims=True) / full.size + EPSILON)
    for part in range(2):
        for m in range(probe.shape[1]):
            new[part, m] = probe[part, m] - scale * total[pl.ds((2 * m + part) * win, win)]
        copy = pltpu.make_async_copy(new.at[part], new_out.at[part], sem.at[2 * count + part])
        copy.start()
        copies.append(copy)
    for copy in copies:
        copy.wait()


def on_device(object_tiles, probe_modes, offsets, amplitude):
    n_row, n_col = lax.axis_size("row"), lax.axis_size("col")
    n_z = n_col // 2
    tile, win, scans = object_tiles.shape[2], probe_modes.shape[2], offsets.shape[2]
    tall, nt = tile + 2 * HALO, tile // LANES
    modes = probe_modes.shape[1]
    g_rows = 2 * modes * win
    size = g_rows // CHUNKS
    chunks = tuple((i * size, size) for i in range(CHUNKS))
    piece = g_rows // 2 // n_row
    vmem = pl.BlockSpec(memory_space=pltpu.VMEM)
    hbm = pl.BlockSpec(memory_space=pltpu.HBM)
    dma = pltpu.SemaphoreType.DMA
    block = lambda *shape: pltpu.VMEM(shape, F32)
    pairs = offsets.transpose(0, 1, 3, 2)
    table = jnp.asarray(tables(win))
    grad, total, probe = pl.pallas_call(
        functools.partial(fused_kernel, (n_row, n_col, win, scans, chunks)),
        out_shape=(
            jax.ShapeDtypeStruct(object_tiles.shape, F32),
            jax.ShapeDtypeStruct((g_rows, win), F32),
            jax.ShapeDtypeStruct(probe_modes.shape, F32),
        ),
        in_specs=[hbm] * 5,
        out_specs=(vmem, vmem, vmem),
        scratch_shapes=[
            pltpu.SMEM(pairs.shape, jnp.int32),
            block(2, nt + 1, tall, LANES),
            block(2, nt + 1, tall, LANES),
            block(*amplitude.shape),
            pltpu.VMEM(table.shape, BF16),
            block(scans, 4, win, win),
            block(scans, 2, 2 * win, 2 * win),
            block(scans, 2, 2 * win, 2 * win),
            block(scans, win, win),
            block(2, 2, scans, win, win),
            block(g_rows, win),
            block(scans, 2, nt + 1, 2 * tall - win, LANES),
            block(2, 2, nt + 1, tall, LANES),
            block(2, tile // 2, LANES),
            block(2, tile // 2, LANES),
            block(2, tall // 2, LANES),
            block(2, tall // 2, LANES),
            block(2, 2, nt, HALO, LANES),
            block(2, 2, nt, HALO, LANES),
            block(2, tall // 2, LANES),
            block(2, tall // 2, LANES),
            block(2, tall // 2, LANES),
            block(2, tall // 2, LANES),
            block(g_rows // 2, win),
            block(g_rows // 2, win),
            block(n_row - 1, piece, win),
            block(n_z, piece, win),
            dma((4 * nt + 4,)),
            dma((2, 8)),
            dma((2, 8)),
            dma((2, 8)),
            dma((2, 8)),
            dma((CHUNKS,)),
            dma((CHUNKS,)),
            dma((CHUNKS, n_row - 1)),
            dma((CHUNKS, n_row - 1)),
            dma((CHUNKS, n_z - 1)),
            dma((CHUNKS, n_z - 1)),
            dma((CHUNKS, n_row - 1)),
            dma((CHUNKS, n_row - 1)),
            dma((CHUNKS, n_row)),
            dma((CHUNKS, n_row)),
        ],
        compiler_params=pltpu.CompilerParams(
            collective_id=0, has_side_effects=True, vmem_limit_bytes=48 * 1024 * 1024
        ),
    )(
        *[
            pltpu.with_memory_space_constraint(x, pltpu.HBM)
            for x in (pairs, object_tiles, probe_modes, amplitude, table)
        ],
    )
    return pl.pallas_call(
        out_kernel,
        out_shape=(
            jax.ShapeDtypeStruct(object_tiles.shape, F32),
            jax.ShapeDtypeStruct(probe_modes.shape, F32),
        ),
        in_specs=[vmem, vmem, vmem],
        out_specs=(hbm, hbm),
        scratch_shapes=[block(*probe_modes.shape), dma((2 * object_tiles.shape[1] + 2,))],
        compiler_params=pltpu.CompilerParams(vmem_limit_bytes=4 * 1024 * 1024),
    )(grad, total, probe)


CHUNKS = 2


def solution(mesh):
    placed = (
        P(None, None, "row", "col"),
        P(),
        P("row", "col", None, None),
        P("row", "col", None, None, None),
    )
    return jax.shard_map(
        on_device,
        mesh=mesh,
        in_specs=placed,
        out_specs=(P(None, None, "row", "col"), P()),
        check_vma=False,
    )
```

```python
import functools

import jax
import jax.numpy as jnp
import numpy as np
from jax import lax
from jax.experimental import pallas as pl
from jax.experimental.pallas import tpu as pltpu
from jax.sharding import PartitionSpec as P

HALO = 32
PROP = 0.002
SHIFT_AMP = 0.5
STEP_SIZE = 0.5
EPSILON = 1e-06
LANES = 128
SUB = 8
MESH = pl.DeviceIdType.MESH
F32 = jnp.float32
BF16 = jnp.bfloat16


def tables(win):
    k = np.arange(win)
    c = np.exp(-2j * np.pi * (k[:, None] * k[None, :] % win) / win) / np.sqrt(win)
    freq = (k + win // 2) % win - win // 2
    kern = np.conj(c) @ np.diag(np.exp(-1j * PROP * freq**2)) @ c
    out = []
    for m in (c, np.conj(c), kern, np.conj(kern)):
        full = np.block([[m.real, m.imag], [-m.imag, m.real]])
        high = full.astype(np.float32).astype(jnp.bfloat16)
        low = (full - high.astype(np.float64)).astype(np.float32).astype(jnp.bfloat16)
        out += [high, low]
    return np.stack(out)


FWD, INV, KER, KER_INV = 0, 1, 2, 3


def split(x):
    high = x.astype(BF16)
    return high, (x - high.astype(F32)).astype(BF16)


def dot(a, b):
    return jnp.dot(a, b, preferred_element_type=F32)


def right(x, tab, which):
    high, low = split(x)
    return dot(high, tab[2 * which]) + (
        dot(low, tab[2 * which]) + dot(high, tab[2 * which + 1])
    )


def left(x, tab, which):
    high, low = split(x)
    which = which ^ 1
    return dot(tab[2 * which], high) + (
        dot(tab[2 * which], low) + dot(tab[2 * which + 1], high)
    )


def swap(y):
    w = y.shape[0] // 2
    top = jnp.concatenate([y[:w, :w], y[w:, :w]], axis=1)
    low = jnp.concatenate([y[:w, w:], y[w:, w:]], axis=1)
    return jnp.concatenate([top, low], axis=0)


def twice(x, axis):
    return jnp.concatenate([x, x], axis=axis)


def lane(rows):
    return lax.broadcasted_iota(jnp.int32, (rows, LANES), 1)


FOLD = HALO // 2


def fold(get, rows, first):
    at = lane(rows // 2)
    out = None
    for part in range(2):
        x = get(part)
        for h in range(2):
            low = HALO * (2 * h + part)
            block = jnp.concatenate(
                [x[HALO * b + FOLD * h : HALO * b + FOLD * (h + 1)] for b in range(rows // HALO)],
                axis=0,
            )
            shift = (low - first) % LANES
            block = pltpu.roll(block, shift, 1) if shift else block
            keep = (at >= low) & (at < low + HALO)
            out = jnp.where(keep, block, 0.0 if out is None else out)
    return out


def unfold(x, part, first):
    halves = []
    for h in range(2):
        shift = (first - HALO * (2 * h + part)) % LANES
        halves.append(pltpu.roll(x, shift, 1) if shift else x)
    return jnp.concatenate(
        [
            halves[h][FOLD * b : FOLD * (b + 1)]
            for b in range(x.shape[0] // FOLD)
            for h in range(2)
        ],
        axis=0,
    )


def remote(src, dst, ssem, rsem, to):
    copy = pltpu.make_async_remote_copy(
        src_ref=src,
        dst_ref=dst,
        send_sem=ssem,
        recv_sem=rsem,
        device_id=to,
        device_id_type=MESH,
    )
    copy.start()
    return copy


def fused_kernel(
    sizes,
    off_hbm,
    obj_hbm,
    probe_hbm,
    amp_hbm,
    tab_hbm,
    grad_ref,
    total,
    probe,
    off_ref,
    ext_0,
    ext_1,
    amp,
    tab,
    winds,
    wave,
    far,
    factor,
    gobj,
    gprobe,
    zpad,
    acc,
    pack_l,
    pack_r,
    halo_l,
    halo_r,
    from_top,
    from_bot,
    edge_l,
    edge_r,
    from_l,
    from_r,
    half_in,
    half_sum,
    r_parts,
    z_parts,
    in_sem,
    h_send,
    h_recv,
    g_send,
    g_recv,
    pair_send,
    pair_recv,
    r_send,
    r_recv,
    z_send,
    z_recv,
    ag_send,
    ag_recv,
    fw_send,
    fw_recv,
):
    n_row, n_col, win, scans, chunks = sizes
    n_z = n_col // 2
    ext = (ext_0, ext_1)
    tile = grad_ref.shape[2]
    tall = tile + 2 * HALO
    nt = tile // LANES
    pad = tall - win
    my_r, my_c = lax.axis_index("row"), lax.axis_index("col")

    def at(dr, dc):
        return lax.rem(my_r + dr % n_row, n_row), lax.rem(my_c + dc % n_col, n_col)

    barrier = pltpu.get_barrier_semaphore()
    mates = {(dr % n_row, dc % n_col) for dr in (-1, 0, 1) for dc in (-1, 0, 1)}
    mates |= {(k, 0) for k in range(n_row)} | {(0, 2 * k) for k in range(n_z)}
    mates.discard((0, 0))
    hops = lambda mate: min(mate[0], n_row - mate[0]) + min(mate[1], n_col - mate[1])
    for mate in sorted(sorted(mates), key=hops, reverse=True):
        pl.semaphore_signal(barrier, inc=1, device_id=at(*mate), device_id_type=MESH)
    loads = []
    for lay in range(2):
        for part in range(2):
            for t in range(nt):
                loads.append(
                    pltpu.make_async_copy(
                        obj_hbm.at[part, lay, :, pl.ds(t * LANES, LANES)],
                        ext[lay].at[part, t, pl.ds(HALO, tile), :],
                        in_sem.at[len(loads)],
                    )
                )
    per_lay = len(loads) // 2
    for src, dst in ((off_hbm, off_ref), (probe_hbm, probe), (tab_hbm, tab), (amp_hbm, amp)):
        loads.append(pltpu.make_async_copy(src, dst, in_sem.at[len(loads)]))
    for load in loads[: 2 * per_lay + 1]:
        load.start()

    head, tail = pl.ds(0, FOLD), pl.ds((tile - HALO) // 2, FOLD)
    mid, after = pl.ds(FOLD, tile // 2), pl.ds(FOLD + tile // 2, FOLD)

    def pack(lay):
        for load in loads[lay * per_lay : (lay + 1) * per_lay]:
            load.wait()
        own = pl.ds(HALO, tile)
        pack_l[lay] = fold(lambda part: ext[lay][part, 0, own, :], tile, 0)
        pack_r[lay] = fold(lambda part: ext[lay][part, nt - 1, own, :], tile, LANES - HALO)

    def halo_start(lay, which):
        e, left_in, right_in = ext[lay], halo_l.at[lay], halo_r.at[lay]
        pl_, pr_ = pack_l.at[lay], pack_r.at[lay]
        own = pl.ds(0, nt)
        plan = [
            (e.at[:, own, pl.ds(tile, HALO)], e.at[:, own, pl.ds(0, HALO)], (1, 0)),
            (e.at[:, own, pl.ds(HALO, HALO)], e.at[:, own, pl.ds(HALO + tile, HALO)], (-1, 0)),
            (pr_, left_in.at[mid], (0, 1)),
            (pl_, right_in.at[mid], (0, -1)),
            (pr_.at[tail], left_in.at[head], (1, 1)),
            (pr_.at[head], left_in.at[after], (-1, 1)),
            (pl_.at[tail], right_in.at[head], (1, -1)),
            (pl_.at[head], right_in.at[after], (-1, -1)),
        ]
        return [
            remote(src, dst, h_send.at[lay, i], h_recv.at[lay, i], at(*to))
            for i, (src, dst, to) in ((i, plan[i]) for i in which)
        ]

    def halo_end(lay, copies, rows):
        for copy in copies:
            copy.wait_recv()
        for part in range(2):
            near = unfold(halo_r[lay], part, 0)
            distant = unfold(halo_l[lay], part, LANES - HALO)
            x = lane(tall)
            ext[lay][part, nt, pl.ds(0, tall), :] = jnp.where(
                x < HALO, near, jnp.where(x >= LANES - HALO, distant, 0.0)
            )
        for copy in rows:
            copy.wait_recv()

    def spot(s):
        row = off_ref[0, 0, 0, s]
        col = off_ref[0, 0, 1, s] - HALO
        col = jnp.where(col < 0, col + (nt + 1) * LANES, col)
        first = lax.div(col, LANES)
        second = jnp.where(first == nt, 0, first + 1)
        return row, first, second, col - first * LANES

    def windows(lay):
        for s in range(scans):
            row, first, second, rem = spot(s)
            for part in range(2):
                a = ext[lay][part, first, pl.ds(row, win), :]
                b = ext[lay][part, second, pl.ds(row, win), :]
                block = jnp.where(lane(win) >= rem, a, b)
                winds[s, 2 * part + lay] = pltpu.roll(block, lax.rem(LANES - rem, LANES), 1)

    sides, ends = (4, 5, 6, 7, 2, 3), (0, 1)
    pack(0)
    pack(1)
    pl.semaphore_wait(barrier, len(mates))
    sides_0 = halo_start(0, sides)
    sides_1 = halo_start(1, sides)
    ends_0 = halo_start(0, ends)
    ends_1 = halo_start(1, ends)
    for load in loads[2 * per_lay + 1 :]:
        load.start()
    gprobe[...] = jnp.zeros_like(gprobe)
    gobj[...] = jnp.zeros_like(gobj)
    zpad[...] = jnp.zeros_like(zpad)
    for load in loads[2 * per_lay :]:
        load.wait()
    halo_end(0, sides_0, ends_0)
    windows(0)

    for s in range(scans):
        or_, oi_ = winds[s, 0], winds[s, 2]
        for p in range(2):
            rows = []
            for m in range(2):
                pr, pi = probe[0, 2 * p + m], probe[1, 2 * p + m]
                rows.append(
                    jnp.concatenate([pr * or_ - pi * oi_, pr * oi_ + pi * or_], axis=1)
                )
            psi = jnp.concatenate(rows, axis=0)
            wave[s, p] = left(swap(right(psi, tab, KER)), tab, KER)

    halo_end(1, sides_1, ends_1)
    windows(1)

    for s in range(scans):
        power = None
        for p in range(2):
            w = wave[s, p]
            wr, wi = w[:win], w[win:]
            o1r, o1i = twice(winds[s, 1], 1), twice(winds[s, 3], 1)
            psi = jnp.concatenate([wr * o1r - wi * o1i, wr * o1i + wi * o1r], axis=0)
            psi = right(swap(left(psi, tab, FWD)), tab, FWD)
            far[s, p] = psi
            sq = psi * psi
            part_sum = (sq[:win, :win] + sq[:win, win:]) + (sq[win:, :win] + sq[win:, win:])
            power = part_sum if power is None else power + part_sum
        root = jnp.sqrt(power + SHIFT_AMP)
        factor[s] = 2.0 * (root - amp[0, 0, s]) / root

    def first_half(p, s):
        g = far[s, p] * twice(twice(factor[s], 0), 1)
        g = left(swap(right(g, tab, INV)), tab, INV)
        w = wave[s, p]
        gr, gi, wr, wi = g[:win], g[win:], w[:win], w[win:]
        re = wr * gr + wi * gi
        im = wr * gi - wi * gr
        gobj[1, 0, s] += re[:, :win] + re[:, win:]
        gobj[1, 1, s] += im[:, :win] + im[:, win:]
        o1r, o1i = twice(winds[s, 1], 1), twice(winds[s, 3], 1)
        far[s, p] = jnp.concatenate([o1r * gr + o1i * gi, o1r * gi - o1i * gr], axis=0)

    def second_half(p, s):
        g = right(swap(left(far[s, p], tab, KER_INV)), tab, KER_INV)
        o0r, o0i = winds[s, 0], winds[s, 2]
        re = im = None
        for m in range(2):
            gr, gi = g[m * win : (m + 1) * win, :win], g[m * win : (m + 1) * win, win:]
            pr, pi = probe[0, 2 * p + m], probe[1, 2 * p + m]
            a = pr * gr + pi * gi
            b = pr * gi - pi * gr
            re, im = (a, b) if re is None else (re + a, im + b)
            base = (2 * p + m) * 2 * win
            gprobe[pl.ds(base, win)] += o0r * gr + o0i * gi
            gprobe[pl.ds(base + win, win)] += o0r * gi - o0i * gr
        gobj[0, 0, s] += re
        gobj[0, 1, s] += im

    def place(lay):
        starts = []
        for s in range(scans):
            row, first, second, rem = spot(s)
            starts.append(pad - row)
            where = jnp.where(lane(win) >= rem, first, second)
            for part in range(2):
                block = pltpu.roll(gobj[lay, part, s], rem, 1)
                for t in range(nt + 1):
                    zpad[lay, s, part, t, pl.ds(pad, win), :] = jnp.where(where == t, block, 0.0)
        return starts

    def gather(lay, starts, tiles):
        for part in range(2):
            for t in tiles:
                value = None
                for s in range(scans):
                    block = zpad[lay, s, part, t, pl.ds(starts[s], tall), :]
                    value = block if value is None else value + block
                acc[lay, part, t] = value

    def grads_fold(lay):
        edge_r[lay] = fold(lambda part: acc[lay, part, nt], tall, 0)
        edge_l[lay] = fold(lambda part: acc[lay, part, nt], tall, LANES - HALO)

    def grads_start(lay, which):
        a, er, el = acc.at[lay], edge_r.at[lay], edge_l.at[lay]
        fl, fr = from_l.at[lay], from_r.at[lay]
        own = pl.ds(0, nt)
        plan = [
            (a.at[:, own, pl.ds(0, HALO)], from_bot.at[lay], (-1, 0)),
            (a.at[:, own, pl.ds(HALO + tile, HALO)], from_top.at[lay], (1, 0)),
            (er.at[mid], fl.at[mid], (0, 1)),
            (el.at[mid], fr.at[mid], (0, -1)),
            (er.at[head], fl.at[after], (-1, 1)),
            (er.at[after], fl.at[head], (1, 1)),
            (el.at[head], fr.at[after], (-1, -1)),
            (el.at[after], fr.at[head], (1, -1)),
        ]
        return [
            remote(src, dst, g_send.at[lay, i], g_recv.at[lay, i], at(*to))
            for i, (src, dst, to) in ((i, plan[i]) for i in which)
        ]

    def grads_end(lay, copies):
        for copy in copies:
            copy.wait_recv()
        x = lane(tall)
        for part in range(2):
            for t in range(nt):
                value = acc[lay, part, t, pl.ds(HALO, tile), :]
                top, bot = from_top[lay, part, t], from_bot[lay, part, t]
                for ref, first, edge in ((from_l, 0, 0), (from_r, LANES - HALO, nt - 1)):
                    if t == edge:
                        block = unfold(ref[lay], part, first)
                        block = jnp.where((x >= first) & (x < first + HALO), block, 0.0)
                        value = value + block[HALO : HALO + tile]
                        top = top + block[:HALO]
                        bot = bot + block[HALO + tile :]
                cols = pl.ds(t * LANES, LANES)
                grad_ref[part, lay, pl.ds(0, HALO), cols] = value[:HALO] + top
                grad_ref[part, lay, pl.ds(HALO, tile - 2 * HALO), cols] = value[HALO:-HALO]
                grad_ref[part, lay, pl.ds(tile - HALO, HALO), cols] = value[-HALO:] + bot

    odd = lax.rem(my_c, 2)
    partner = (my_r, my_c + 1 - 2 * odd)
    my_z = lax.div(my_c, 2)

    def span(c):
        start, size = chunks[c]
        half = size // 2
        piece = half // n_row
        return start, half, piece, start // 2, start // 2 // n_row

    def rows_at(start, size):
        return pl.ds(pl.multiple_of(start, SUB), size)

    def row_mate(k):
        return lax.rem(my_r + k, n_row)

    def pair_start(c):
        start, half, piece, hs, ps = span(c)
        return remote(
            gprobe.at[rows_at(start + (1 - odd) * half, half)],
            half_in.at[pl.ds(hs, half)],
            pair_send.at[c],
            pair_recv.at[c],
            partner,
        )

    def r_start(c, pair):
        start, half, piece, hs, ps = span(c)
        pair.wait_recv()
        half_sum[pl.ds(hs, half)] = (
            gprobe[rows_at(start + odd * half, half)] + half_in[pl.ds(hs, half)]
        )
        copies = []
        for k in range(1, n_row):
            q = row_mate(k)
            copies.append(
                remote(
                    half_sum.at[rows_at(hs + q * piece, piece)],
                    r_parts.at[k - 1, pl.ds(ps, piece)],
                    r_send.at[c, k - 1],
                    r_recv.at[c, k - 1],
                    (q, my_c),
                )
            )
        return copies

    def z_start(c, before):
        start, half, piece, hs, ps = span(c)
        for copy in before:
            copy.wait_recv()
        value = half_sum[rows_at(hs + my_r * piece, piece)]
        for k in range(n_row - 1):
            value = value + r_parts[k, pl.ds(ps, piece)]
        z_parts[my_z, pl.ds(ps, piece)] = value
        mine = z_parts.at[my_z, pl.ds(ps, piece)]
        return [
            remote(mine, mine, z_send.at[c, k - 1], z_recv.at[c, k - 1], at(0, 2 * k))
            for k in range(1, n_z)
        ]

    def ag_start(c, before):
        start, half, piece, hs, ps = span(c)
        for copy in before:
            copy.wait_recv()
        value = z_parts[0, pl.ds(ps, piece)]
        for k in range(1, n_z):
            value = value + z_parts[k, pl.ds(ps, piece)]
        own = rows_at(start + odd * half + my_r * piece, piece)
        total[own] = value
        mine = total.at[own]
        copies = [
            remote(mine, mine, ag_send.at[c, k - 1], ag_recv.at[c, k - 1], at(k, 0))
            for k in range(1, n_row)
        ]
        return copies, [remote(mine, mine, fw_send.at[c, 0], fw_recv.at[c, 0], partner)]

    def fw_start(c, copies, forwards):
        start, half, piece, hs, ps = span(c)
        for k in range(1, n_row):
            copies[k - 1].wait_recv()
            q = lax.rem(my_r + n_row - k, n_row)
            got = total.at[rows_at(start + odd * half + q * piece, piece)]
            forwards.append(remote(got, got, fw_send.at[c, k], fw_recv.at[c, k], partner))

    early, late = range(len(chunks) // 2), range(len(chunks) // 2, len(chunks))
    every = range(len(chunks))
    pair, row, zed, gat = {}, {}, {}, {}
    for s in range(scans):
        first_half(0, s)
    for s in range(scans):
        second_half(0, s)
    for c in early:
        pair[c] = pair_start(c)
    for s in range(scans):
        first_half(1, s)
    starts = place(1)
    gather(1, starts, (nt,))
    grads_fold(1)
    copies_1 = grads_start(1, (4, 5, 6, 7, 2, 3))
    for c in early:
        row[c] = r_start(c, pair[c])
    for s in range(scans):
        second_half(1, s)
    for c in late:
        pair[c] = pair_start(c)
    gather(1, starts, range(nt))
    starts = place(0)
    gather(0, starts, range(nt + 1))
    grads_fold(0)
    copies_0 = grads_start(0, (4, 5, 6, 7, 2, 3))
    for c in late:
        row[c] = r_start(c, pair[c])
    copies_1 += grads_start(1, (0, 1))
    copies_0 += grads_start(0, (0, 1))
    for c in early:
        zed[c] = z_start(c, row[c])
    for c in late:
        zed[c] = z_start(c, row[c])
    for c in early:
        gat[c] = ag_start(c, zed[c])
    for c in late:
        gat[c] = ag_start(c, zed[c])
    grads_end(1, copies_1)
    grads_end(0, copies_0)
    for c in every:
        fw_start(c, *gat[c])
    for copy in sides_0 + ends_0 + sides_1 + ends_1 + copies_0 + copies_1:
        copy.wait_send()
    for c in every:
        for copy in [pair[c]] + row[c] + zed[c] + gat[c][0]:
            copy.wait_send()
    for c in every:
        for copy in gat[c][1]:
            copy.wait()


def out_kernel(grad, total, probe, grad_out, new_out, new, sem):
    count = grad.shape[1]
    copies = [
        pltpu.make_async_copy(grad.at[i, j], grad_out.at[i, j], sem.at[i * count + j])
        for i in range(2)
        for j in range(count)
    ]
    for copy in copies:
        copy.start()
    full = total[...]
    win = probe.shape[2]
    scale = STEP_SIZE / jnp.sqrt(jnp.sum(full * full, keepdims=True) / full.size + EPSILON)
    for part in range(2):
        for m in range(probe.shape[1]):
            new[part, m] = probe[part, m] - scale * total[pl.ds((2 * m + part) * win, win)]
        copy = pltpu.make_async_copy(new.at[part], new_out.at[part], sem.at[2 * count + part])
        copy.start()
        copies.append(copy)
    for copy in copies:
        copy.wait()


def on_device(object_tiles, probe_modes, offsets, amplitude):
    n_row, n_col = lax.axis_size("row"), lax.axis_size("col")
    n_z = n_col // 2
    tile, win, scans = object_tiles.shape[2], probe_modes.shape[2], offsets.shape[2]
    tall, nt = tile + 2 * HALO, tile // LANES
    modes = probe_modes.shape[1]
    g_rows = 2 * modes * win
    size = g_rows // CHUNKS
    chunks = tuple((i * size, size) for i in range(CHUNKS))
    piece = g_rows // 2 // n_row
    vmem = pl.BlockSpec(memory_space=pltpu.VMEM)
    hbm = pl.BlockSpec(memory_space=pltpu.HBM)
    dma = pltpu.SemaphoreType.DMA
    block = lambda *shape: pltpu.VMEM(shape, F32)
    pairs = offsets.transpose(0, 1, 3, 2)
    table = jnp.asarray(tables(win))
    grad, total, probe = pl.pallas_call(
        functools.partial(fused_kernel, (n_row, n_col, win, scans, chunks)),
        out_shape=(
            jax.ShapeDtypeStruct(object_tiles.shape, F32),
            jax.ShapeDtypeStruct((g_rows, win), F32),
            jax.ShapeDtypeStruct(probe_modes.shape, F32),
        ),
        in_specs=[hbm] * 5,
        out_specs=(vmem, vmem, vmem),
        scratch_shapes=[
            pltpu.SMEM(pairs.shape, jnp.int32),
            block(2, nt + 1, tall, LANES),
            block(2, nt + 1, tall, LANES),
            block(*amplitude.shape),
            pltpu.VMEM(table.shape, BF16),
            block(scans, 4, win, win),
            block(scans, 2, 2 * win, 2 * win),
            block(scans, 2, 2 * win, 2 * win),
            block(scans, win, win),
            block(2, 2, scans, win, win),
            block(g_rows, win),
            block(2, scans, 2, nt + 1, 2 * tall - win, LANES),
            block(2, 2, nt + 1, tall, LANES),
            block(2, tile // 2, LANES),
            block(2, tile // 2, LANES),
            block(2, tall // 2, LANES),
            block(2, tall // 2, LANES),
            block(2, 2, nt, HALO, LANES),
            block(2, 2, nt, HALO, LANES),
            block(2, tall // 2, LANES),
            block(2, tall // 2, LANES),
            block(2, tall // 2, LANES),
            block(2, tall // 2, LANES),
            block(g_rows // 2, win),
            block(g_rows // 2, win),
            block(n_row - 1, piece, win),
            block(n_z, piece, win),
            dma((4 * nt + 4,)),
            dma((2, 8)),
            dma((2, 8)),
            dma((2, 8)),
            dma((2, 8)),
            dma((CHUNKS,)),
            dma((CHUNKS,)),
            dma((CHUNKS, n_row - 1)),
            dma((CHUNKS, n_row - 1)),
            dma((CHUNKS, n_z - 1)),
            dma((CHUNKS, n_z - 1)),
            dma((CHUNKS, n_row - 1)),
            dma((CHUNKS, n_row - 1)),
            dma((CHUNKS, n_row)),
            dma((CHUNKS, n_row)),
        ],
        compiler_params=pltpu.CompilerParams(
            collective_id=0, has_side_effects=True, vmem_limit_bytes=48 * 1024 * 1024
        ),
    )(
        *[
            pltpu.with_memory_space_constraint(x, pltpu.HBM)
            for x in (pairs, object_tiles, probe_modes, amplitude, table)
        ],
    )
    return pl.pallas_call(
        out_kernel,
        out_shape=(
            jax.ShapeDtypeStruct(object_tiles.shape, F32),
            jax.ShapeDtypeStruct(probe_modes.shape, F32),
        ),
        in_specs=[vmem, vmem, vmem],
        out_specs=(hbm, hbm),
        scratch_shapes=[block(*probe_modes.shape), dma((2 * object_tiles.shape[1] + 2,))],
        compiler_params=pltpu.CompilerParams(vmem_limit_bytes=4 * 1024 * 1024),
    )(grad, total, probe)


CHUNKS = 2


def solution(mesh):
    placed = (
        P(None, None, "row", "col"),
        P(),
        P("row", "col", None, None),
        P("row", "col", None, None, None),
    )
    return jax.shard_map(
        on_device,
        mesh=mesh,
        in_specs=placed,
        out_specs=(P(None, None, "row", "col"), P()),
        check_vma=False,
    )
```
